128 devices in a mesh: owner: 32 (over z, y, core), sub: 4 (over x).
Axes of the slice: x: 4, y: 4, z: 4, core: 2. Of those that a mesh axis runs over, the one named last changes fastest.
Arguments:
- velocity: float32 [6, 65536], P(None, 'owner'), may hold values from -6 to 6
- properties: float32 [4, 65536], P(None, 'owner'), may hold values from 0.3 to 3
- first_body: int32 [4194304], P(('owner', 'sub')), may hold values from 0 to 65535, as said below
- second_body: int32 [4194304], P(('owner', 'sub')), may hold values from 0 to 65535, as said below
- geometry: float32 [9, 4194304], P(None, ('owner', 'sub')), may hold values from -2 to 2, as said below
- target_speed: float32 [4194304], P(('owner', 'sub')), may hold values from -1 to 2
- warm_impulse: float32 [4194304], P(('owner', 'sub')), may hold values from 0 to 0.5
- live_pairs: int32 [32768], P(('owner', 'sub')), may hold values from 0 to 128, as said below
Outputs:
- velocity_out: float32 [6, 65536], P(None, 'owner')
- impulse_out: float32 [4194304], P(('owner', 'sub'))
The draws below stay inside these ranges and needn't reach their ends.
Inputs may be any that keep to these rules, and one draw needn't show every extreme that they name: Pair slots are ordered by device of owner+sub, then by partner owner, then by 8 blocks of 128 slots; a slot on a device of owner o with partner owner q has first_body in [o * 2048, (o+1) * 2048) and second_body in [q * 2048, (q+1) * 2048). `second_body`: see first_body. `live_pairs`: on every device the first block toward its own owner is full; live counts differ strongly between devices and between partner owners. `geometry`: rows 0 to 2 of every column have unit length.
All inputs are finite; a program needn't handle non-finite values.
Results may differ from the reference program's by a relative error of at most 0.0001.
Values sent between devices are 32-bit elements; how exact they have to be, the bound alone decides.
No kernel may reach another device: no remote copies, remote signals or barrier semaphores. Data moves between devices by JAX's collectives and lax.ppermute only.
A program may use at most 128 MiB of HBM per device.

```python
import math
import jax
import jax.numpy as jnp

B_OWN = 2048
KB = 8
PAIR = 128
ITERS = 4
BODIES = 65536
PAIRS = 4194304
BLOCKS = 32768
N_OWNER = 32
N_SUB = 4


def slot_owners():
    slots = jnp.arange(PAIRS, dtype=jnp.int32)
    owner_of = slots // (N_OWNER * KB * PAIR * N_SUB)
    partner = slots // (KB * PAIR) % N_OWNER
    return (owner_of, partner)


def draw_first_body(key, part):
    owner_of, partner = slot_owners()
    return owner_of * B_OWN + jax.random.randint(jax.random.fold_in(key, 11), (PAIRS,), 0, B_OWN, dtype=jnp.int32)


def draw_second_body(key, part):
    owner_of, partner = slot_owners()
    return partner * B_OWN + jax.random.randint(jax.random.fold_in(key, 12), (PAIRS,), 0, B_OWN, dtype=jnp.int32)


def draw_live_pairs(key, part):
    blocks = jnp.arange(BLOCKS, dtype=jnp.int32)
    per_device = N_OWNER * KB
    device = blocks // per_device
    owner_of = device // N_SUB
    partner = blocks // KB % N_OWNER
    apart = jnp.abs(partner - owner_of)
    apart = jnp.minimum(apart, N_OWNER - apart)
    near = (apart <= 1) | (apart == 4)
    level = jax.random.randint(jax.random.fold_in(key, 21), (N_OWNER * N_SUB,), 1, 5, dtype=jnp.int32)[device]
    near_counts = jax.random.randint(jax.random.fold_in(key, 22), (BLOCKS,), PAIR // 2, PAIR + 1, dtype=jnp.int32)
    far_counts = jax.random.randint(jax.random.fold_in(key, 23), (BLOCKS,), 0, PAIR // 4 + 1, dtype=jnp.int32)
    far_counts = jnp.minimum(far_counts * level // 2, PAIR)
    counts = jnp.where(near, near_counts, far_counts)
    own_first = (partner == owner_of) & (blocks % KB == 0)
    return jnp.where(own_first, PAIR, counts).astype(jnp.int32)


def draw_geometry(key, part):
    angle = jax.random.uniform(jax.random.fold_in(key, 31), (PAIRS,), jnp.float32, -3.14159, 3.14159)
    height = jax.random.uniform(jax.random.fold_in(key, 32), (PAIRS,), jnp.float32, -1.0, 1.0)
    radial = jnp.sqrt(jnp.maximum(1.0 - height * height, 0.0))
    normal = jnp.stack([radial * jnp.cos(angle), radial * jnp.sin(angle), height])
    arms = jax.random.uniform(jax.random.fold_in(key, 33), (6, PAIRS), jnp.float32, -1.0, 1.0)
    return jnp.concatenate([normal, arms]).astype(jnp.float32)


def levels(rng, dims, split, low, high):
    gain, own = 1.0, jax.random.fold_in(rng, 6)
    for dim, parts in split:
        draws = jnp.exp(jax.random.uniform(jax.random.fold_in(own, dim), (parts,), jnp.float32, low / len(split), high / len(split)))
        gain = gain * jnp.repeat(draws, dims[dim] // parts).reshape([-1 if axis == dim else 1 for axis in range(len(dims))])
    return gain


def normal_values(rng, dims, width, most, shards=(), held_as=jnp.bfloat16):
    values = jax.random.normal(rng, dims, jnp.float32) * width
    if len(shards) > 0:
        values = levels(rng, dims, shards, -0.22, 0.18) * values
    return jnp.clip(values, min=-most, max=most).astype(held_as)


def setup_inputs(seed: int = 0) -> dict:
    seeds = jax.random.split(jax.random.key(seed), 9)
    return {
        "velocity": normal_values(seeds[0], (6, BODIES), 1.0, 6.0, ((1, 32),), jnp.float32),
        "properties": jnp.clip(jnp.exp(math.log(3.0) - 2.3025851 * jax.random.uniform(seeds[1], (4, BODIES), jnp.float32) ** levels(seeds[1], (4, BODIES), ((1, 32),), -0.2, 0.2)), 0.3, 3.0),
        "first_body": draw_first_body(jax.random.fold_in(seeds[8], 71), 0),
        "second_body": draw_second_body(jax.random.fold_in(seeds[8], 71), 0),
        "geometry": draw_geometry(jax.random.fold_in(seeds[8], 71), 0),
        "target_speed": jnp.clip(-1.0 + 3.0 * jax.random.uniform(seeds[5], (PAIRS,), jnp.float32) ** levels(seeds[5], (PAIRS,), ((0, 128),), -0.2, 0.2), -1.0, 2.0),
        "warm_impulse": jnp.clip(0.5 * jax.random.uniform(seeds[6], (PAIRS,), jnp.float32) ** levels(seeds[6], (PAIRS,), ((0, 128),), -0.2, 0.2), 0.0, 0.5),
        "live_pairs": draw_live_pairs(jax.random.fold_in(seeds[8], 71), 0),
    }


relax = 0.1


def cross_rows(left, right):
    return jnp.stack([left[1] * right[2] - left[2] * right[1],
                      left[2] * right[0] - left[0] * right[2],
                      left[0] * right[1] - left[1] * right[0]])


def reference(velocity, properties, first_body, second_body, geometry, target_speed, warm_impulse, live_pairs):
    slots = jnp.arange(PAIRS, dtype=jnp.int32)
    live = (slots % PAIR) < jnp.repeat(live_pairs, PAIR, total_repeat_length=PAIRS)
    normal = geometry[0:3]
    arm_first = geometry[3:6]
    arm_second = geometry[6:9]
    cross_first = cross_rows(arm_first, normal)
    cross_second = cross_rows(arm_second, normal)
    props_first = properties[:, first_body]
    props_second = properties[:, second_body]
    mass_sum = props_first[0] + props_second[0] + jnp.sum(cross_first * cross_first * props_first[1:4], 0) + jnp.sum(cross_second * cross_second * props_second[1:4], 0)
    speeds = velocity
    impulse = warm_impulse
    for iteration in range(ITERS):
        vel_first = speeds[:, first_body]
        vel_second = speeds[:, second_body]
        relative = vel_first[0:3] + cross_rows(vel_first[3:6], arm_first) - vel_second[0:3] - cross_rows(vel_second[3:6], arm_second)
        normal_speed = jnp.sum(normal * relative, 0)
        change = relax * (target_speed - normal_speed) / mass_sum
        fresh = jnp.where(live, jnp.maximum(impulse + change, 0.0), impulse)
        applied = fresh - impulse
        impulse = fresh
        delta_first = jnp.concatenate([props_first[0] * applied * normal, props_first[1:4] * (applied * cross_first)])
        delta_second = -jnp.concatenate([props_second[0] * applied * normal, props_second[1:4] * (applied * cross_second)])
        total = jnp.zeros(speeds.shape, jnp.float32).at[:, first_body].add(delta_first).at[:, second_body].add(delta_second)
        speeds = speeds + total
    return speeds, impulse
```

```python
import functools

import jax
import jax.numpy as jnp
from jax import lax
from jax.experimental import pallas as pl
from jax.experimental.pallas import tpu as pltpu
from jax.sharding import PartitionSpec as P

ITERS = 4
relax = 0.1
F32 = jnp.float32
BF16 = jnp.bfloat16
LANES = 128
BLK = 8
PEERS = 32
HIGH = 16
ROWS = PEERS * BLK
STREAM = ROWS + BLK
PARAMS = pltpu.CompilerParams(vmem_limit_bytes=40 << 20)
VMEM = pl.BlockSpec(memory_space=pltpu.VMEM)
SMEM = pl.BlockSpec(memory_space=pltpu.SMEM)


def lane_iota():
    return lax.broadcasted_iota(jnp.int32, (8, LANES), 1)


def row_iota():
    return lax.broadcasted_iota(jnp.int32, (8, LANES), 0)


def pack_kernel(live, geom, first, second, target, warm, send, local, mixed, packed0, packed1):
    lanes = lane_iota()
    subs = row_iota()
    dead = jnp.where(subs == 4, -1.0, 0.0).astype(F32)

    def one_partner(q, _):
        rows = pl.ds(pl.multiple_of(q * BLK, BLK), BLK)
        mixed[pl.ds(4, 8, stride=8), :] = (second[rows, :] & (HIGH * LANES - 1)).astype(F32)
        mixed[pl.ds(5, 8, stride=8), :] = warm[rows, :]
        mixed[pl.ds(6, 8, stride=8), :] = target[rows, :]
        mixed[pl.ds(7, 8, stride=8), :] = (first[rows, :] & (HIGH * LANES - 1)).astype(F32)
        cols = [pl.ds(pl.multiple_of(q * BLK * LANES + b * LANES, LANES), LANES) for b in range(BLK)]
        for b in range(BLK):
            mixed[pl.ds(8 * b + 3, 1), :] = geom[8:9, cols[b]]
        offset = jnp.int32(0)
        cur0 = jnp.zeros((8, LANES), F32)
        cur1 = cur0
        for b in range(BLK):
            geo = geom[0:8, cols[b]]
            mix = mixed[8 * b : 8 * b + 8, :]
            shift = offset & (LANES - 1)
            row = offset >> 7
            rolled0 = pltpu.roll(jnp.where((subs >= 3) & (subs < 6), mix, geo), shift, 1)
            rolled1 = pltpu.roll(jnp.where(subs >= 6, mix, geo), shift, 1)
            keep = lanes < shift
            cur0 = jnp.where(keep, cur0, rolled0)
            cur1 = jnp.where(keep, cur1, rolled1)
            packed0[row] = cur0
            packed1[row] = cur1
            offset = offset + live[q * BLK + b]
            spill = jnp.broadcast_to((offset >> 7) > row, (8, LANES))
            cur0 = jnp.where(spill, rolled0, cur0)
            cur1 = jnp.where(spill, rolled1, cur1)
        packed0[offset >> 7] = cur0
        packed1[offset >> 7] = cur1
        for r in range(BLK):
            alive = lanes + r * LANES < offset
            send[q, 8 * r : 8 * r + 8, :] = jnp.where(alive, packed0[r], dead)
            local[q, 8 * r : 8 * r + 8, :] = jnp.where(alive, packed1[r], 0.0)
        return 0

    lax.fori_loop(0, PEERS, one_partner, 0)


def gather_rows(tables, index, count):
    lows = [i & (LANES - 1) for i in index]
    highs = [i >> 7 for i in index]
    found = [[None] * count for _ in index]
    for h in range(HIGH):
        masks = [hi == h for hi in highs]
        for c in range(count):
            ref, start = tables[c]
            line = jnp.broadcast_to(ref[start + h : start + h + 1, :], (8, LANES))
            for k in range(len(index)):
                got = jnp.take_along_axis(line, lows[k], axis=1, mode="promise_in_bounds")
                found[k][c] = got if h == 0 else jnp.where(masks[k], got, found[k][c])
    return found


def group_rows(g):
    return pl.ds(pl.multiple_of(g * 8, 8), 8)


def prepare(first, meta, d0, d1, vel, prop, x_out, idx_out, imp_out, u_out, m_out):
    total = meta[PEERS]

    def one_group(g, _):
        base = g * 64

        def get(ref, k):
            return ref[pl.ds(base + k, 8, stride=8), :]

        flag = get(d0, 4)
        alive = (flag >= 0.0) & (row_iota() + g * 8 < total)
        if first:
            normal = [get(d1, k) for k in (0, 1, 2)]
            arm = [get(d1, k) for k in (3, 4, 5)]
            index = get(d1, 7)
            sign = 1.0
        else:
            normal = [get(d0, k) for k in (0, 1, 2)]
            arm = [get(d0, k) for k in (6, 7, 3)]
            index = flag
            sign = -1.0
        cross = [
            arm[1] * normal[2] - arm[2] * normal[1],
            arm[2] * normal[0] - arm[0] * normal[2],
            arm[0] * normal[1] - arm[1] * normal[0],
        ]
        index = jnp.where(alive, index, 0.0).astype(jnp.int32)
        tables = [(vel, 16 * c) for c in range(6)] + [(prop, 16 * c) for c in range(4)]
        got = gather_rows(tables, [index], 10)[0]
        terms = [jnp.where(alive, sign * t, 0.0) for t in normal + cross]
        mass = got[6]
        for k in range(3):
            mass = mass + cross[k] * cross[k] * got[7 + k]
        u = terms[0] * got[0]
        for c in range(1, 6):
            u = u + terms[c] * got[c]
        for c in range(6):
            x_out[g, c] = terms[c]
        if first:
            off = jnp.where(alive, get(d1, 6), 0.0)
            x_out[g, 6] = off
            u = u - off
        rows = group_rows(g)
        idx_out[rows, :] = index
        imp_out[rows, :] = jnp.where(alive, get(d0, 5), 0.0)
        u_out[rows, :] = u
        m_out[rows, :] = jnp.where(alive, mass, -1.0)
        return 0

    lax.fori_loop(0, (total + 7) >> 3, one_group, 0)


def first_kernel(
    live, send, local, velocity, properties,
    x_out, idx_out, imp_out, u_out, m_out, meta, share, vel, prop, d0, d1,
):
    for c in range(6):
        for h in range(HIGH):
            vel[c * HIGH + h : c * HIGH + h + 1, :] = velocity[c : c + 1, h * LANES : (h + 1) * LANES]
    for c in range(4):
        for h in range(HIGH):
            prop[c * HIGH + h : c * HIGH + h + 1, :] = properties[c : c + 1, h * LANES : (h + 1) * LANES]

    def one_partner(q, base):
        count = live[q * BLK]
        for b in range(1, BLK):
            count = count + live[q * BLK + b]
        meta[q] = base
        rows = pl.ds(pl.multiple_of(base * 8, 8), 64)
        d0[rows, :] = send[q]
        d1[rows, :] = local[q]
        return base + ((count + LANES - 1) >> 7)

    meta[PEERS] = lax.fori_loop(0, PEERS, one_partner, jnp.int32(0))
    prepare(True, meta, d0, d1, vel, prop, x_out, idx_out, imp_out, u_out, m_out)

    def one_share(q, _):
        rows = pl.ds(meta[q], 8)
        share[q, 0] = u_out[rows, :]
        share[q, 1] = m_out[rows, :]
        return 0

    lax.fori_loop(0, PEERS, one_share, 0)


def second_kernel(
    received, share_first, vel, prop,
    x_out, idx_out, imp_out, u_out, m_out, meta, share, d0,
):
    def one_partner(q, base):
        meta[q] = base
        block = received[q]
        d0[pl.ds(pl.multiple_of(base * 8, 8), 64), :] = block
        flags = received[q, pl.ds(4, 8, stride=8), :]
        used = jnp.max(jnp.where(flags >= 0.0, row_iota() + 1, 0))
        return base + used

    meta[PEERS] = lax.fori_loop(0, PEERS, one_partner, jnp.int32(0))
    prepare(False, meta, d0, None, vel, prop, x_out, idx_out, imp_out, u_out, m_out)

    def one_share(q, _):
        rows = pl.ds(meta[q], 8)
        share[q, 0] = share_first[q, 0]
        share[q, 1] = share_first[q, 1]
        share[q, 2] = u_out[rows, :]
        share[q, 3] = m_out[rows, :]
        return 0

    lax.fori_loop(0, PEERS, one_share, 0)


def apply_kernel(start, *refs):
    (meta_a, meta_b, x_a, x_b, idx_a, idx_b, imp_a, imp_b, u_a, u_b, w_a, w_b, received) = refs[:13]
    outs = refs[13:]
    if start:
        j_out, new_a, new_b, weight_a, weight_b, other_a, other_b, mass_a, mass_b, total = outs
    else:
        j_out, new_a, new_b, other_a, other_b, total = outs
        weight_a, weight_b, mass_a, mass_b = w_a, w_b, None, None

    step = 2 if start else 1

    def one_partner(p, _):
        rows_a = pl.ds(meta_a[p], 8)
        rows_b = pl.ds(meta_b[p], 8)
        other_a[rows_a, :] = received[p, step]
        other_b[rows_b, :] = received[p, 0]
        if start:
            mass_a[rows_a, :] = received[p, 3]
            mass_b[rows_b, :] = received[p, 1]
        return 0

    lax.fori_loop(0, PEERS, one_partner, 0)
    total[...] = jnp.zeros_like(total)
    iota_high = lax.broadcasted_iota(jnp.int32, (HIGH, LANES), 0)
    iota_low = lax.broadcasted_iota(jnp.int32, (LANES, LANES), 0)

    def side(x, idx, imp, u, other, mass, own_mass, weight, new):
        def one_group(g, _):
            rows = group_rows(g)
            if mass is not None:
                mine = own_mass[rows, :]
                alive = mine > 0.0
                scale = jnp.where(alive, relax / (mine + mass[rows, :]), 0.0)
                weight[rows, :] = scale
            else:
                scale = weight[rows, :]
                alive = scale > 0.0
            before = imp[rows, :]
            fresh = jnp.maximum(before - (u[rows, :] + other[rows, :]) * scale, 0.0)
            fresh = jnp.where(alive, fresh, before)
            applied = fresh - before
            new[rows, :] = fresh
            values = [applied * x[g, c] for c in range(6)]
            tops = [v.astype(BF16).astype(F32) for v in values]
            pieces = tops + [v - t for v, t in zip(values, tops)]
            index = idx[rows, :]
            low = index & (LANES - 1)
            high = index >> 7
            lefts = []
            rights = []
            for b in range(8):
                mask = jnp.broadcast_to(high[b : b + 1], (HIGH, LANES)) == iota_high
                lefts.append(
                    jnp.concatenate(
                        [
                            jnp.where(mask, jnp.broadcast_to(v[b : b + 1], (HIGH, LANES)), 0.0).astype(BF16)
                            for v in pieces
                        ],
                        axis=0,
                    )
                )
                hit = jnp.broadcast_to(low[b : b + 1], (LANES, LANES)) == iota_low
                rights.append(jnp.where(hit, 1.0, 0.0).astype(BF16))
            total[...] += lax.dot_general(
                jnp.concatenate(lefts, axis=1),
                jnp.concatenate(rights, axis=1),
                (((1,), (1,)), ((), ())),
                preferred_element_type=F32,
            )
            return 0

        return one_group

    lax.fori_loop(
        0, (meta_a[PEERS] + 7) >> 3,
        side(x_a, idx_a, imp_a, u_a, other_a, mass_a, w_a, weight_a, new_a), 0,
    )
    lax.fori_loop(
        0, (meta_b[PEERS] + 7) >> 3,
        side(x_b, idx_b, imp_b, u_b, other_b, mass_b, w_b, weight_b, new_b), 0,
    )
    j_out[...] = total[0:96] + total[96:192]


def moved(vel, prop, j0, j1, j2, j3, c):
    rows = slice(c * HIGH, (c + 1) * HIGH)
    k = max(c - 2, 0)
    gain = (j0[rows, :] + j2[rows, :]) + (j1[rows, :] + j3[rows, :])
    return vel[rows, :] + prop[k * HIGH : (k + 1) * HIGH, :] * gain


def gather_kernel(
    meta_a, meta_b, vel, prop, j0, j1, j2, j3, x_a, x_b, idx_a, idx_b,
    vel_out, u_a, u_b, share,
):
    for c in range(6):
        vel_out[c * HIGH : (c + 1) * HIGH, :] = moved(vel, prop, j0, j1, j2, j3, c)
    tables = [(vel_out, HIGH * c) for c in range(6)]

    def side(x, idx, u_out, offset):
        def two_groups(pair, _):
            groups = [pair * 2, pair * 2 + 1]
            got = gather_rows(tables, [idx[group_rows(g), :] for g in groups], 6)
            for k, g in enumerate(groups):
                u = x[g, 0] * got[k][0]
                for c in range(1, 6):
                    u = u + x[g, c] * got[k][c]
                if offset:
                    u = u - x[g, 6]
                u_out[group_rows(g), :] = u
            return 0

        return two_groups

    lax.fori_loop(0, (meta_a[PEERS] + 15) >> 4, side(x_a, idx_a, u_a, True), 0)
    lax.fori_loop(0, (meta_b[PEERS] + 15) >> 4, side(x_b, idx_b, u_b, False), 0)

    def one_share(q, _):
        share[q, 0] = u_a[pl.ds(meta_a[q], 8), :]
        share[q, 1] = u_b[pl.ds(meta_b[q], 8), :]
        return 0

    lax.fori_loop(0, PEERS, one_share, 0)


def final_kernel(vel, prop, j0, j1, j2, j3, out):
    for c in range(6):
        rows = moved(vel, prop, j0, j1, j2, j3, c)
        for h in range(HIGH):
            out[c : c + 1, h * LANES : (h + 1) * LANES] = rows[h : h + 1]


def unpack_kernel(live, meta, imp, warm, out):
    lanes = lax.broadcasted_iota(jnp.int32, (1, LANES), 1)

    def one_partner(q, _):
        offset = jnp.int32(0)
        for b in range(BLK):
            count = live[q * BLK + b]
            shift = offset & (LANES - 1)
            row = meta[q] + (offset >> 7)
            here = imp[pl.ds(row, 1), :]
            after = imp[pl.ds(row + 1, 1), :]
            both = jnp.where(lanes >= shift, here, after)
            back = pltpu.roll(both, (LANES - shift) & (LANES - 1), 1)
            slot = pl.ds(q * BLK + b, 1)
            out[slot, :] = jnp.where(lanes < count, back, warm[slot, :])
            offset = offset + count
        return 0

    lax.fori_loop(0, PEERS, one_partner, 0)


def shape(*dims, dtype=F32):
    return jax.ShapeDtypeStruct(dims, dtype)


def call(kernel, ins, outs, scratch=(), flops=10_000_000, bytes_accessed=4_000_000, name=None):
    return pl.pallas_call(
        kernel,
        in_specs=list(ins),
        out_specs=tuple(SMEM if o.dtype == jnp.int32 and len(o.shape) == 1 else VMEM for o in outs),
        out_shape=tuple(outs),
        scratch_shapes=list(scratch),
        compiler_params=PARAMS,
        cost_estimate=pl.CostEstimate(
            flops=flops, bytes_accessed=bytes_accessed, transcendentals=0
        ),
        name=name,
    )


def on_device(
    velocity, properties, first_body, second_body, geometry, target_speed, warm_impulse, live_pairs
):
    table = lambda array: array.reshape(ROWS, LANES)
    warm = table(warm_impulse)
    stream = shape(STREAM, LANES)
    meta_shape = shape(PEERS + 1, dtype=jnp.int32)
    send, local = call(
        pack_kernel,
        [SMEM] + [VMEM] * 5,
        [shape(PEERS, 64, LANES)] * 2,
        [pltpu.VMEM((64, LANES), F32)] + [pltpu.VMEM((16, 8, LANES), F32)] * 2,
        name="pack",
    )(live_pairs, geometry, table(first_body), table(second_body), table(target_speed), warm)
    received = lax.all_to_all(send, "owner", split_axis=0, concat_axis=0, tiled=True)
    x_a, idx_a, imp_a, u_a, m_a, meta_a, share_a, vel, prop = call(
        first_kernel,
        [SMEM] + [VMEM] * 4,
        [
            shape(ROWS // 8, 7, 8, LANES), shape(STREAM, LANES, dtype=jnp.int32), stream, stream,
            stream, meta_shape, shape(PEERS, 2, 8, LANES), shape(96, LANES), shape(64, LANES),
        ],
        [pltpu.VMEM((STREAM * 8, LANES), F32)] * 2,
        name="first",
    )(live_pairs, send, local, velocity, properties)
    x_b, idx_b, imp_b, u_b, m_b, meta_b, share = call(
        second_kernel,
        [VMEM] * 4,
        [
            shape(ROWS // 8, 6, 8, LANES), shape(STREAM, LANES, dtype=jnp.int32), stream, stream,
            stream, meta_shape, shape(PEERS, 4, 8, LANES),
        ],
        [pltpu.VMEM((STREAM * 8, LANES), F32)],
        name="second",
    )(received, share_a, vel, prop)
    w_a, w_b = m_a, m_b
    n_sub = lax.axis_size("sub")
    for iteration in range(ITERS):
        start = iteration == 0
        told = lax.all_to_all(share, "owner", split_axis=0, concat_axis=0, tiled=True)
        outs = call(
            functools.partial(apply_kernel, start),
            [SMEM, SMEM] + [VMEM] * 11,
            [shape(96, LANES), stream, stream] + ([stream, stream] if start else []),
            [pltpu.VMEM((STREAM, LANES), F32)] * (4 if start else 2)
            + [pltpu.VMEM((192, LANES), F32)],
            name="apply",
        )(meta_a, meta_b, x_a, x_b, idx_a, idx_b, imp_a, imp_b, u_a, u_b, w_a, w_b, told)
        if start:
            own, imp_a, imp_b, w_a, w_b = outs
        else:
            own, imp_a, imp_b = outs
        gains = [own] + [
            lax.ppermute(own, "sub", [(i, (i + d) % n_sub) for i in range(n_sub)])
            for d in (1, 2, 3)
        ]
        if iteration < ITERS - 1:
            vel, u_a, u_b, share = call(
                gather_kernel,
                [SMEM, SMEM] + [VMEM] * 10,
                [shape(96, LANES), stream, stream, shape(PEERS, 2, 8, LANES)],
                name="gather",
            )(meta_a, meta_b, vel, prop, *gains, x_a, x_b, idx_a, idx_b)
    (impulse,) = call(
        unpack_kernel, [SMEM, SMEM, VMEM, VMEM], [shape(ROWS, LANES)], name="unpack"
    )(live_pairs, meta_a, imp_a, warm)
    (out,) = call(final_kernel, [VMEM] * 6, [shape(6, HIGH * LANES)], name="final")(
        vel, prop, *gains
    )
    return (out, impulse.reshape(-1))


def solution(mesh):
    return jax.shard_map(
        on_device,
        mesh=mesh,
        in_specs=(
            P(None, "owner"),
            P(None, "owner"),
            P(("owner", "sub")),
            P(("owner", "sub")),
            P(None, ("owner", "sub")),
            P(("owner", "sub")),
            P(("owner", "sub")),
            P(("owner", "sub")),
        ),
        out_specs=(P(None, "owner"), P(("owner", "sub"))),
        check_vma=False,
    )
```

```python
import functools

import jax
import jax.numpy as jnp
from jax import lax
from jax.experimental import pallas as pl
from jax.experimental.pallas import tpu as pltpu
from jax.sharding import PartitionSpec as P

ITERS = 4
relax = 0.1
F32 = jnp.float32
BF16 = jnp.bfloat16
LANES = 128
BLK = 8
PEERS = 32
HIGH = 16
ROWS = PEERS * BLK
STAGE = ROWS + 2 * BLK
CHUNK = 4
GROUPS = 2 * ROWS // 8 + CHUNK
STREAM = GROUPS * 8
COUNT = 2 * PEERS
PART = 4
VMEM = pl.BlockSpec(memory_space=pltpu.VMEM)
SMEM = pl.BlockSpec(memory_space=pltpu.SMEM)


def lane_iota():
    return lax.broadcasted_iota(jnp.int32, (8, LANES), 1)


def row_iota():
    return lax.broadcasted_iota(jnp.int32, (8, LANES), 0)


def pack_kernel(live, geom, first, second, target, warm, send, local, mixed, packed0, packed1):
    start = pl.program_id(0) * PART
    lanes = lane_iota()
    subs = row_iota()
    dead = jnp.where(subs == 4, -1.0, 0.0).astype(F32)

    def one_partner(q, _):
        rows = pl.ds(pl.multiple_of(q * BLK, BLK), BLK)
        mixed[pl.ds(4, 8, stride=8), :] = (second[rows, :] & (HIGH * LANES - 1)).astype(F32)
        mixed[pl.ds(5, 8, stride=8), :] = warm[rows, :]
        mixed[pl.ds(6, 8, stride=8), :] = target[rows, :]
        mixed[pl.ds(7, 8, stride=8), :] = (first[rows, :] & (HIGH * LANES - 1)).astype(F32)
        cols = [pl.ds(pl.multiple_of(q * BLK * LANES + b * LANES, LANES), LANES) for b in range(BLK)]
        for b in range(BLK):
            mixed[pl.ds(8 * b + 3, 1), :] = geom[8:9, cols[b]]
        offset = jnp.int32(0)
        cur0 = jnp.zeros((8, LANES), F32)
        cur1 = cur0
        for b in range(BLK):
            geo = geom[0:8, cols[b]]
            mix = mixed[8 * b : 8 * b + 8, :]
            shift = offset & (LANES - 1)
            row = offset >> 7
            rolled0 = pltpu.roll(jnp.where((subs >= 3) & (subs < 6), mix, geo), shift, 1)
            rolled1 = pltpu.roll(jnp.where(subs >= 6, mix, geo), shift, 1)
            keep = lanes < shift
            cur0 = jnp.where(keep, cur0, rolled0)
            cur1 = jnp.where(keep, cur1, rolled1)
            packed0[row] = cur0
            packed1[row] = cur1
            offset = offset + live[(start + q) * BLK + b]
            spill = jnp.broadcast_to((offset >> 7) > row, (8, LANES))
            cur0 = jnp.where(spill, rolled0, cur0)
            cur1 = jnp.where(spill, rolled1, cur1)
        packed0[offset >> 7] = cur0
        packed1[offset >> 7] = cur1
        for r in range(BLK):
            alive = lanes + r * LANES < offset
            send[q, 8 * r : 8 * r + 8, :] = jnp.where(alive, packed0[r], dead)
            local[q, 8 * r : 8 * r + 8, :] = jnp.where(alive, packed1[r], 0.0)
        return 0

    lax.fori_loop(0, PART, one_partner, 0)


def gather_rows(tables, index, count):
    lows = [i & (LANES - 1) for i in index]
    highs = [i >> 7 for i in index]
    found = [[None] * count for _ in index]
    for h in range(HIGH):
        masks = [hi == h for hi in highs]
        for c in range(count):
            ref, start = tables[c]
            line = jnp.broadcast_to(ref[start + h : start + h + 1, :], (8, LANES))
            for k in range(len(index)):
                got = jnp.take_along_axis(line, lows[k], axis=1, mode="promise_in_bounds")
                found[k][c] = got if h == 0 else jnp.where(masks[k], got, found[k][c])
    return found


def group_rows(g):
    return pl.ds(pl.multiple_of(g * 8, 8), 8)


def prepare(first, shift, total, d0, d1, vel, prop, x_out, idx_out, imp_out, u_out, m_out):
    def load(g):
        base = g * 64

        def get(ref, k):
            return ref[pl.ds(base + k, 8, stride=8), :]

        flag = get(d0, 4)
        alive = (flag >= 0.0) & (row_iota() + g * 8 < total)
        source, arms, index = (d1, (3, 4, 5), get(d1, 7)) if first else (d0, (6, 7, 3), flag)
        normal = [get(source, k) for k in (0, 1, 2)]
        arm = [get(source, k) for k in arms]
        cross = [
            arm[1] * normal[2] - arm[2] * normal[1],
            arm[2] * normal[0] - arm[0] * normal[2],
            arm[0] * normal[1] - arm[1] * normal[0],
        ]
        return get, alive, jnp.where(alive, index, 0.0).astype(jnp.int32), normal, cross

    def two_groups(pair, _):
        groups = [pair * 2, pair * 2 + 1]
        indices = [load(g)[2] for g in groups]
        masses = gather_rows([(prop, HIGH * c) for c in range(4)], indices, 4)
        for k, g in enumerate(groups):
            get, alive, index, normal, cross = load(g)
            mass = masses[k][0]
            for c in range(3):
                mass = mass + cross[c] * cross[c] * masses[k][1 + c]
            rows = group_rows(g + shift)
            m_out[rows, :] = jnp.where(alive, mass, -1.0)
            idx_out[rows, :] = index
            imp_out[rows, :] = jnp.where(alive, get(d0, 5), 0.0)
            sign = 1.0 if first else -1.0
            for c, term in enumerate(normal + cross):
                x_out[g + shift, c] = jnp.where(alive, sign * term, 0.0)
            x_out[g + shift, 6] = (
                jnp.where(alive, get(d1, 6), 0.0) if first else jnp.zeros((8, LANES), F32)
            )
        project(groups, shift, vel, x_out, idx_out, u_out)
        return 0

    lax.fori_loop(0, (total + 15) >> 4, two_groups, 0)


def project(groups, shift, vel, x, idx, u_out):
    rows = [group_rows(g + shift) for g in groups]
    got = gather_rows([(vel, HIGH * c) for c in range(6)], [idx[r, :] for r in rows], 6)
    for k, g in enumerate(groups):
        u = x[g + shift, 0] * got[k][0]
        for c in range(1, 6):
            u = u + x[g + shift, c] * got[k][c]
        u_out[rows[k], :] = u - x[g + shift, 6]


def first_kernel(
    live, send, local, velocity, properties,
    x_out, idx_out, imp_out, u_out, m_out, meta, share, vel, prop, d0, d1,
):
    for c in range(6):
        for h in range(HIGH):
            vel[c * HIGH + h : c * HIGH + h + 1, :] = velocity[c : c + 1, h * LANES : (h + 1) * LANES]
    for c in range(4):
        for h in range(HIGH):
            prop[c * HIGH + h : c * HIGH + h + 1, :] = properties[c : c + 1, h * LANES : (h + 1) * LANES]

    def one_partner(q, base):
        count = live[q * BLK]
        for b in range(1, BLK):
            count = count + live[q * BLK + b]
        meta[q] = base
        rows = pl.ds(pl.multiple_of(base * 8, 8), 64)
        d0[rows, :] = send[q]
        d1[rows, :] = local[q]
        return base + ((count + LANES - 1) >> 7)

    total = lax.fori_loop(0, PEERS, one_partner, jnp.int32(0))
    meta[PEERS] = total
    prepare(True, 0, total, d0, d1, vel, prop, x_out, idx_out, imp_out, u_out, m_out)

    def one_share(q, _):
        rows = pl.ds(meta[q], 8)
        share[q, 0] = u_out[rows, :]
        share[q, 1] = m_out[rows, :]
        return 0

    lax.fori_loop(0, PEERS, one_share, 0)


def second_kernel(
    received, share_first, vel, prop, meta_first, x_in, idx_in, imp_in, u_in, m_in,
    x_out, idx_out, imp_out, u_out, m_out, meta, share, d0, used,
):
    def count_rows(q, _):
        flags = received[q, pl.ds(4, 8, stride=8), :]
        used[q] = jnp.max(jnp.where(flags >= 0.0, row_iota() + 1, 0))
        return 0

    lax.fori_loop(0, PEERS, count_rows, 0, unroll=8)
    shift = (meta_first[PEERS] + 7) >> 3

    def one_partner(q, base):
        meta[q] = meta_first[q]
        meta[PEERS + q] = base + shift * 8
        d0[pl.ds(pl.multiple_of(base * 8, 8), 64), :] = received[q]
        return base + used[q]

    total = lax.fori_loop(0, PEERS, one_partner, jnp.int32(0))
    groups = shift + ((total + 7) >> 3)
    meta[COUNT] = groups
    prepare(False, shift, total, d0, None, vel, prop, x_out, idx_out, imp_out, u_out, m_out)
    zero = jnp.zeros((8, LANES), F32)
    for k in range(CHUNK):
        rows = group_rows(groups + k)
        for c in range(7):
            x_out[groups + k, c] = zero
        idx_out[rows, :] = zero.astype(jnp.int32)
        imp_out[rows, :] = zero
        u_out[rows, :] = zero
        m_out[rows, :] = zero - 1.0

    def one_share(q, _):
        rows = pl.ds(meta[PEERS + q], 8)
        share[q, 0] = share_first[q, 0]
        share[q, 1] = share_first[q, 1]
        share[q, 2] = u_out[rows, :]
        share[q, 3] = m_out[rows, :]
        return 0

    lax.fori_loop(0, PEERS, one_share, 0)


def apply_kernel(start, meta, x, idx, imp, u, w, received, *refs):
    if start:
        j_out, new, weight, other, mass = refs
    else:
        j_out, new, other = refs
        weight = w
    step = 2 if start else 1

    def one_partner(p, _):
        other[pl.ds(meta[p], 8), :] = received[p, step]
        if start:
            mass[pl.ds(meta[p], 8), :] = received[p, 3]
        return 0

    def second_partner(p, _):
        other[pl.ds(meta[PEERS + p], 8), :] = received[p, 0]
        if start:
            mass[pl.ds(meta[PEERS + p], 8), :] = received[p, 1]
        return 0

    lax.fori_loop(0, PEERS, one_partner, 0)
    lax.fori_loop(0, PEERS, second_partner, 0)
    iota_high = lax.broadcasted_iota(jnp.int32, (HIGH, LANES), 0)
    iota_low = lax.broadcasted_iota(jnp.int32, (LANES, LANES), 0)

    def one_chunk(i, total):
        lefts = []
        rights = []
        for j in range(CHUNK):
            g = i * CHUNK + j
            rows = group_rows(g)
            if start:
                mine = w[rows, :]
                alive = mine > 0.0
                scale = jnp.where(alive, relax / (mine + mass[rows, :]), 0.0)
                weight[rows, :] = scale
            else:
                scale = weight[rows, :]
                alive = scale > 0.0
            before = imp[rows, :]
            fresh = jnp.maximum(before - (u[rows, :] + other[rows, :]) * scale, 0.0)
            fresh = jnp.where(alive, fresh, before)
            applied = fresh - before
            new[rows, :] = fresh
            values = [applied * x[g, c] for c in range(6)]
            tops = [v.astype(BF16).astype(F32) for v in values]
            pieces = tops + [v - t for v, t in zip(values, tops)]
            index = idx[rows, :]
            low = index & (LANES - 1)
            high = index >> 7
            for b in range(8):
                mask = jnp.broadcast_to(high[b : b + 1], (HIGH, LANES)) == iota_high
                lefts.append(
                    jnp.concatenate(
                        [
                            jnp.where(mask, jnp.broadcast_to(v[b : b + 1], (HIGH, LANES)), 0.0).astype(BF16)
                            for v in pieces
                        ],
                        axis=0,
                    )
                )
                hit = jnp.broadcast_to(low[b : b + 1], (LANES, LANES)) == iota_low
                rights.append(jnp.where(hit, 1.0, 0.0).astype(BF16))
        return total + lax.dot_general(
            jnp.concatenate(lefts, axis=1),
            jnp.concatenate(rights, axis=1),
            (((1,), (1,)), ((), ())),
            preferred_element_type=F32,
        )

    chunks = (meta[COUNT] + CHUNK - 1) // CHUNK
    total = lax.fori_loop(0, chunks, one_chunk, jnp.zeros((12 * HIGH, LANES), F32))
    j_out[...] = total[0:96] + total[96:192]


def moved(vel, prop, j0, j1, j2, j3, c):
    rows = slice(c * HIGH, (c + 1) * HIGH)
    k = max(c - 2, 0)
    gain = (j0[rows, :] + j2[rows, :]) + (j1[rows, :] + j3[rows, :])
    return vel[rows, :] + prop[k * HIGH : (k + 1) * HIGH, :] * gain


def gather_kernel(meta, vel, prop, j0, j1, j2, j3, x, idx, vel_out, u_out, share):
    for c in range(6):
        vel_out[c * HIGH : (c + 1) * HIGH, :] = moved(vel, prop, j0, j1, j2, j3, c)

    def two_groups(pair, _):
        project([pair * 2, pair * 2 + 1], 0, vel_out, x, idx, u_out)
        return 0

    lax.fori_loop(0, (meta[COUNT] + 1) >> 1, two_groups, 0)

    def one_share(q, _):
        share[q, 0] = u_out[pl.ds(meta[q], 8), :]
        share[q, 1] = u_out[pl.ds(meta[PEERS + q], 8), :]
        return 0

    lax.fori_loop(0, PEERS, one_share, 0)


def final_kernel(vel, prop, j0, j1, j2, j3, out):
    for c in range(6):
        rows = moved(vel, prop, j0, j1, j2, j3, c)
        for h in range(HIGH):
            out[c : c + 1, h * LANES : (h + 1) * LANES] = rows[h : h + 1]


def unpack_kernel(live, meta, imp, warm, out):
    lanes = lax.broadcasted_iota(jnp.int32, (1, LANES), 1)

    def one_partner(q, _):
        offset = jnp.int32(0)
        for b in range(BLK):
            count = live[q * BLK + b]
            shift = offset & (LANES - 1)
            row = meta[q] + (offset >> 7)
            here = imp[pl.ds(row, 1), :]
            after = imp[pl.ds(row + 1, 1), :]
            both = jnp.where(lanes >= shift, here, after)
            back = pltpu.roll(both, (LANES - shift) & (LANES - 1), 1)
            slot = pl.ds(q * BLK + b, 1)
            out[slot, :] = jnp.where(lanes < count, back, warm[slot, :])
            offset = offset + count
        return 0

    lax.fori_loop(0, PEERS, one_partner, 0, unroll=2)


def shape(*dims, dtype=F32):
    return jax.ShapeDtypeStruct(dims, dtype)


def call(kernel, ins, outs, scratch=(), aliases=None, name=None):
    return pl.pallas_call(
        kernel,
        in_specs=list(ins),
        out_specs=tuple(SMEM if o.dtype == jnp.int32 and len(o.shape) == 1 else VMEM for o in outs),
        out_shape=tuple(outs),
        scratch_shapes=list(scratch),
        input_output_aliases=aliases or {},
        compiler_params=pltpu.CompilerParams(vmem_limit_bytes=16 << 20),
        cost_estimate=pl.CostEstimate(
            flops=10_000_000, bytes_accessed=4_000_000, transcendentals=0
        ),
        name=name,
    )


def pack(live, geometry, first, second, target, warm):
    rows = pl.BlockSpec((PART * BLK, LANES), lambda i: (i, 0))
    out = pl.BlockSpec((PART, 64, LANES), lambda i: (i, 0, 0))
    return pl.pallas_call(
        pack_kernel,
        grid=(PEERS // PART,),
        in_specs=[SMEM, pl.BlockSpec((9, PART * BLK * LANES), lambda i: (0, i))] + [rows] * 4,
        out_specs=(out, out),
        out_shape=(shape(PEERS, 64, LANES),) * 2,
        scratch_shapes=[pltpu.VMEM((64, LANES), F32)] + [pltpu.VMEM((16, 8, LANES), F32)] * 2,
        compiler_params=pltpu.CompilerParams(
            dimension_semantics=("arbitrary",), vmem_limit_bytes=60 << 20
        ),
        name="pack",
    )(live, geometry, first, second, target, warm)


def on_device(
    velocity, properties, first_body, second_body, geometry, target_speed, warm_impulse, live_pairs
):
    table = lambda array: array.reshape(ROWS, LANES)
    warm = table(warm_impulse)
    stream = shape(STREAM, LANES)
    streams = [
        shape(GROUPS, 7, 8, LANES), shape(STREAM, LANES, dtype=jnp.int32), stream, stream, stream
    ]
    send, local = pack(
        live_pairs, geometry, table(first_body), table(second_body), table(target_speed), warm
    )
    received = lax.all_to_all(send, "owner", split_axis=0, concat_axis=0, tiled=True)
    x, idx, imp, u, m, meta_first, share, vel, prop = call(
        first_kernel,
        [SMEM] + [VMEM] * 4,
        streams
        + [
            shape(PEERS + 1, dtype=jnp.int32), shape(PEERS, 2, 8, LANES),
            shape(96, LANES), shape(64, LANES),
        ],
        [pltpu.VMEM((STAGE * 8, LANES), F32)] * 2,
        name="first",
    )(live_pairs, send, local, velocity, properties)
    x, idx, imp, u, m, meta, share = call(
        second_kernel,
        [VMEM] * 4 + [SMEM] + [VMEM] * 5,
        streams + [shape(COUNT + 1, dtype=jnp.int32), shape(PEERS, 4, 8, LANES)],
        [pltpu.VMEM((STAGE * 8, LANES), F32), pltpu.SMEM((PEERS,), jnp.int32)],
        aliases={5 + k: k for k in range(5)},
        name="second",
    )(received, share, vel, prop, meta_first, x, idx, imp, u, m)
    weight = m
    n_sub = lax.axis_size("sub")
    for iteration in range(ITERS):
        start = iteration == 0
        told = lax.all_to_all(share, "owner", split_axis=0, concat_axis=0, tiled=True)
        outs = call(
            functools.partial(apply_kernel, start),
            [SMEM] + [VMEM] * 6,
            [shape(96, LANES), stream] + ([stream] if start else []),
            [pltpu.VMEM((STREAM, LANES), F32)] * (2 if start else 1),
            name="apply",
        )(meta, x, idx, imp, u, weight, told)
        own, imp = outs[:2]
        if start:
            weight = outs[2]
        gains = [own] + [
            lax.ppermute(own, "sub", [(i, (i + d) % n_sub) for i in range(n_sub)])
            for d in (1, 2, 3)
        ]
        if iteration < ITERS - 1:
            vel, u, share = call(
                gather_kernel,
                [SMEM] + [VMEM] * 8,
                [shape(96, LANES), stream, shape(PEERS, 2, 8, LANES)],
                name="gather",
            )(meta, vel, prop, *gains, x, idx)
    (impulse,) = call(
        unpack_kernel, [SMEM, SMEM, VMEM, VMEM], [shape(ROWS, LANES)], name="unpack"
    )(live_pairs, meta, imp, warm)
    (out,) = call(final_kernel, [VMEM] * 6, [shape(6, HIGH * LANES)], name="final")(
        vel, prop, *gains
    )
    return (out, impulse.reshape(-1))


def solution(mesh):
    return jax.shard_map(
        on_device,
        mesh=mesh,
        in_specs=(
            P(None, "owner"),
            P(None, "owner"),
            P(("owner", "sub")),
            P(("owner", "sub")),
            P(None, ("owner", "sub")),
            P(("owner", "sub")),
            P(("owner", "sub")),
            P(("owner", "sub")),
        ),
        out_specs=(P(None, "owner"), P(("owner", "sub"))),
        check_vma=False,
    )
```

```python
import functools

import jax
import jax.numpy as jnp
from jax import lax
from jax.experimental import pallas as pl
from jax.experimental.pallas import tpu as pltpu
from jax.sharding import PartitionSpec as P

ITERS = 4
relax = 0.1
F32 = jnp.float32
BF16 = jnp.bfloat16
LANES = 128
BLK = 8
PEERS = 32
HIGH = 16
ROWS = PEERS * BLK
STAGE = ROWS + 2 * BLK
HALF = float(1 << 20)
CHUNK = 6
GROUPS = 2 * ROWS // 8 + CHUNK
STREAM = GROUPS * 8
COUNT = 2 * PEERS
PART = 8
VMEM = pl.BlockSpec(memory_space=pltpu.VMEM)
SMEM = pl.BlockSpec(memory_space=pltpu.SMEM)


def lane_iota():
    return lax.broadcasted_iota(jnp.int32, (8, LANES), 1)


def row_iota():
    return lax.broadcasted_iota(jnp.int32, (8, LANES), 0)


def pack_kernel(live, geom, first, second, target, warm, send, local, *scratch):
    start = pl.program_id(0) * PART
    lanes = lane_iota()
    subs = row_iota()
    dead = jnp.where(subs == 4, -1.0, 0.0).astype(F32)

    def one_partner(q, mixed, packed0, packed1):
        rows = pl.ds(pl.multiple_of(q * BLK, BLK), BLK)
        mixed[pl.ds(4, 8, stride=8), :] = (second[rows, :] & (HIGH * LANES - 1)).astype(F32)
        mixed[pl.ds(5, 8, stride=8), :] = warm[rows, :]
        mixed[pl.ds(6, 8, stride=8), :] = target[rows, :]
        mixed[pl.ds(7, 8, stride=8), :] = (first[rows, :] & (HIGH * LANES - 1)).astype(F32)
        cols = [pl.ds(pl.multiple_of(q * BLK * LANES + b * LANES, LANES), LANES) for b in range(BLK)]
        for b in range(BLK):
            mixed[pl.ds(8 * b + 3, 1), :] = geom[8:9, cols[b]]
        offset = jnp.int32(0)
        cur0 = jnp.zeros((8, LANES), F32)
        cur1 = cur0
        for b in range(BLK):
            geo = geom[0:8, cols[b]]
            mix = mixed[8 * b : 8 * b + 8, :]
            shift = offset & (LANES - 1)
            row = offset >> 7
            rolled0 = pltpu.roll(jnp.where((subs >= 3) & (subs < 6), mix, geo), shift, 1)
            rolled1 = pltpu.roll(jnp.where(subs >= 6, mix, geo), shift, 1)
            keep = lanes < shift
            cur0 = jnp.where(keep, cur0, rolled0)
            cur1 = jnp.where(keep, cur1, rolled1)
            packed0[row] = cur0
            packed1[row] = cur1
            offset = offset + live[(start + q) * BLK + b]
            spill = jnp.broadcast_to((offset >> 7) > row, (8, LANES))
            cur0 = jnp.where(spill, rolled0, cur0)
            cur1 = jnp.where(spill, rolled1, cur1)
        packed0[offset >> 7] = cur0
        packed1[offset >> 7] = cur1
        for r in range(BLK):
            alive = lanes + r * LANES < offset
            send[q, 8 * r : 8 * r + 8, :] = jnp.where(alive, packed0[r], dead)
            local[q, 8 * r : 8 * r + 8, :] = jnp.where(alive, packed1[r], 0.0)

    def two_partners(pair, _):
        one_partner(pair * 2, *scratch[0::2])
        one_partner(pair * 2 + 1, *scratch[1::2])
        return 0

    lax.fori_loop(0, PART // 2, two_partners, 0)


def gather_rows(tables, index, count):
    lows = [i & (LANES - 1) for i in index]
    highs = [i >> 7 for i in index]
    found = [[None] * count for _ in index]
    for h in range(HIGH):
        masks = [hi == h for hi in highs]
        for c in range(count):
            ref, start = tables[c]
            line = jnp.broadcast_to(ref[start + h : start + h + 1, :], (8, LANES))
            for k in range(len(index)):
                got = jnp.take_along_axis(line, lows[k], axis=1, mode="promise_in_bounds")
                found[k][c] = got if h == 0 else jnp.where(masks[k], got, found[k][c])
    return found


def group_rows(g):
    return pl.ds(pl.multiple_of(g * 8, 8), 8)


def fixed_words(rows, words):
    most = jnp.abs(rows[0])
    for part in rows[1:]:
        most = jnp.maximum(most, jnp.abs(part))
    most = jnp.max(jnp.max(most, axis=0, keepdims=True), axis=1, keepdims=True)
    most = jnp.maximum(jnp.broadcast_to(most, (HIGH, LANES)), 1e-30)
    scale = (HALF - 2.0) / most
    whole = [(part * scale + (HALF + 0.5)).astype(jnp.int32) for part in rows]
    for k in range(4):
        extra = whole[4 + k // 2]
        extra = extra >> 11 if k % 2 else extra & 2047
        words[k * HIGH : (k + 1) * HIGH, :] = whole[k] | (extra << 21)
    return most[0:8] * (1.0 / (HALF - 2.0))


def project(groups, words, unit, x, idx, u_out, offset):
    rows = [group_rows(g) for g in groups]
    got = gather_rows([(words, HIGH * k) for k in range(4)], [idx[r, :] for r in rows], 4)
    for k, g in enumerate(groups):
        tops = [lax.shift_right_logical(w, 21) for w in got[k]]
        whole = [w & ((1 << 21) - 1) for w in got[k]]
        whole += [tops[0] | (tops[1] << 11), tops[2] | (tops[3] << 11)]
        u = jnp.zeros((8, LANES), F32)
        for c in range(6):
            u = u + x[g, c] * (whole[c] - (1 << 20)).astype(F32)
        u = u * unit
        u_out[rows[k], :] = u - x[g, 6] if offset else u


def prepare(first, total, d0, d1, vel, prop, words, x_out, idx_out, imp_out, u_out, m_out):
    unit = fixed_words([vel[c * HIGH : (c + 1) * HIGH, :] for c in range(6)], words)

    def load(g):
        base = g * 64

        def get(ref, k):
            return ref[pl.ds(base + k, 8, stride=8), :]

        flag = get(d0, 4)
        alive = (flag >= 0.0) & (row_iota() + g * 8 < total)
        source, arms, index = (d1, (3, 4, 5), get(d1, 7)) if first else (d0, (6, 7, 3), flag)
        normal = [get(source, k) for k in (0, 1, 2)]
        arm = [get(source, k) for k in arms]
        cross = [
            arm[1] * normal[2] - arm[2] * normal[1],
            arm[2] * normal[0] - arm[0] * normal[2],
            arm[0] * normal[1] - arm[1] * normal[0],
        ]
        return get, alive, jnp.where(alive, index, 0.0).astype(jnp.int32), normal, cross

    def two_groups(pair, _):
        groups = [pair * 2, pair * 2 + 1]
        indices = [load(g)[2] for g in groups]
        masses = gather_rows([(prop, HIGH * c) for c in range(4)], indices, 4)
        for k, g in enumerate(groups):
            get, alive, index, normal, cross = load(g)
            mass = masses[k][0]
            for c in range(3):
                mass = mass + cross[c] * cross[c] * masses[k][1 + c]
            rows = group_rows(g)
            m_out[rows, :] = jnp.where(alive, mass, -1.0)
            idx_out[rows, :] = index
            imp_out[rows, :] = jnp.where(alive, get(d0, 5), 0.0)
            sign = 1.0 if first else -1.0
            for c, term in enumerate(normal + cross):
                x_out[g, c] = jnp.where(alive, sign * term, 0.0)
            if first:
                x_out[g, 6] = jnp.where(alive, get(d1, 6), 0.0)
        project(groups, words, unit, x_out, idx_out, u_out, first)
        return 0

    lax.fori_loop(0, (total + 15) >> 4, two_groups, 0)


def first_kernel(
    live, send, local, velocity, properties,
    x_out, idx_out, imp_out, u_out, m_out, meta, share, vel, prop, d0, d1, words,
):
    for c in range(6):
        for h in range(HIGH):
            vel[c * HIGH + h : c * HIGH + h + 1, :] = velocity[c : c + 1, h * LANES : (h + 1) * LANES]
    for c in range(4):
        for h in range(HIGH):
            prop[c * HIGH + h : c * HIGH + h + 1, :] = properties[c : c + 1, h * LANES : (h + 1) * LANES]

    def one_partner(q, base):
        count = live[q * BLK]
        for b in range(1, BLK):
            count = count + live[q * BLK + b]
        meta[q] = base
        rows = pl.ds(pl.multiple_of(base * 8, 8), 64)
        d0[rows, :] = send[q]
        d1[rows, :] = local[q]
        return base + ((count + LANES - 1) >> 7)

    total = lax.fori_loop(0, PEERS, one_partner, jnp.int32(0))
    meta[PEERS] = total
    prepare(True, total, d0, d1, vel, prop, words, x_out, idx_out, imp_out, u_out, m_out)

    def one_share(q, _):
        rows = pl.ds(meta[q], 8)
        share[q, 0] = u_out[rows, :]
        share[q, 1] = m_out[rows, :]
        return 0

    lax.fori_loop(0, PEERS, one_share, 0)


def second_kernel(
    received, share_first, vel, prop,
    x_out, idx_out, imp_out, u_out, m_out, meta, share, d0, words, used,
):
    def count_rows(q, _):
        flags = received[q, pl.ds(4, 8, stride=8), :]
        used[q] = jnp.max(jnp.where(flags >= 0.0, row_iota() + 1, 0))
        return 0

    lax.fori_loop(0, PEERS, count_rows, 0, unroll=8)

    def one_partner(q, base):
        meta[q] = base
        d0[pl.ds(pl.multiple_of(base * 8, 8), 64), :] = received[q]
        return base + used[q]

    total = lax.fori_loop(0, PEERS, one_partner, jnp.int32(0))
    meta[PEERS] = total
    prepare(False, total, d0, None, vel, prop, words, x_out, idx_out, imp_out, u_out, m_out)

    def one_share(q, _):
        rows = pl.ds(meta[q], 8)
        share[q, 0] = share_first[q, 0]
        share[q, 1] = share_first[q, 1]
        share[q, 2] = u_out[rows, :]
        share[q, 3] = m_out[rows, :]
        return 0

    lax.fori_loop(0, PEERS, one_share, 0)


def merge(side, shift, meta_in, ins, outs):
    terms = 6 if side else 7

    def one_group(g, _):
        for c in range(7):
            outs[0][g + shift, c] = ins[0][g, c] if c < terms else jnp.zeros((8, LANES), F32)
        for k in range(1, 5):
            outs[k][group_rows(g + shift), :] = ins[k][group_rows(g), :]
        return 0

    count = (meta_in[PEERS] + 7) >> 3
    lax.fori_loop(0, count, one_group, 0)
    return shift + count


def apply_kernel(start, *refs):
    if start:
        meta_a, meta_b = refs[:2]
        sides = refs[2:7], refs[7:12]
        received, j_out, new, weight, x, idx, meta, imp, u, w, other, mass = refs[12:]
        shift = merge(0, 0, meta_a, sides[0], (x, idx, imp, u, w))
        groups = merge(1, shift, meta_b, sides[1], (x, idx, imp, u, w))
        meta[COUNT] = groups
        zero = jnp.zeros((8, LANES), F32)
        for k in range(CHUNK):
            rows = group_rows(groups + k)
            for c in range(7):
                x[groups + k, c] = zero
            idx[rows, :] = zero.astype(jnp.int32)
            imp[rows, :] = zero
            u[rows, :] = zero
            w[rows, :] = zero - 1.0
    else:
        meta, x, idx, imp, u, weight, received, j_out, new, other = refs
    step = 2 if start else 1

    def one_partner(p, _):
        if start:
            meta[p] = meta_a[p]
            mass[pl.ds(meta[p], 8), :] = received[p, 3]
        other[pl.ds(meta[p], 8), :] = received[p, step]
        return 0

    def second_partner(p, _):
        if start:
            meta[PEERS + p] = meta_b[p] + shift * 8
            mass[pl.ds(meta[PEERS + p], 8), :] = received[p, 1]
        other[pl.ds(meta[PEERS + p], 8), :] = received[p, 0]
        return 0

    lax.fori_loop(0, PEERS, one_partner, 0)
    lax.fori_loop(0, PEERS, second_partner, 0)
    iota_high = lax.broadcasted_iota(jnp.int32, (HIGH, LANES), 0)
    iota_low = lax.broadcasted_iota(jnp.int32, (LANES, LANES), 0)

    def one_chunk(i, total):
        lefts = []
        rights = []
        for j in range(CHUNK):
            g = i * CHUNK + j
            rows = group_rows(g)
            if start:
                mine = w[rows, :]
                alive = mine > 0.0
                scale = jnp.where(alive, relax / (mine + mass[rows, :]), 0.0)
                weight[rows, :] = scale
            else:
                scale = weight[rows, :]
                alive = scale > 0.0
            before = imp[rows, :]
            fresh = jnp.maximum(before - (u[rows, :] + other[rows, :]) * scale, 0.0)
            fresh = jnp.where(alive, fresh, before)
            applied = fresh - before
            new[rows, :] = fresh
            values = [applied * x[g, c] for c in range(6)]
            tops = [v.astype(BF16).astype(F32) for v in values]
            pieces = tops + [v - t for v, t in zip(values, tops)]
            index = idx[rows, :]
            low = index & (LANES - 1)
            high = index >> 7
            for b in range(8):
                mask = jnp.broadcast_to(high[b : b + 1], (HIGH, LANES)) == iota_high
                lefts.append(
                    jnp.concatenate(
                        [
                            jnp.where(mask, jnp.broadcast_to(v[b : b + 1], (HIGH, LANES)), 0.0).astype(BF16)
                            for v in pieces
                        ],
                        axis=0,
                    )
                )
                hit = jnp.broadcast_to(low[b : b + 1], (LANES, LANES)) == iota_low
                rights.append(jnp.where(hit, 1.0, 0.0).astype(BF16))
        return total + lax.dot_general(
            jnp.concatenate(lefts, axis=1),
            jnp.concatenate(rights, axis=1),
            (((1,), (1,)), ((), ())),
            preferred_element_type=F32,
        )

    chunks = (meta[COUNT] + CHUNK - 1) // CHUNK
    total = lax.fori_loop(0, chunks, one_chunk, jnp.zeros((12 * HIGH, LANES), F32))
    j_out[...] = total[0:96] + total[96:192]


def moved(vel, prop, j0, j1, j2, j3, c):
    rows = slice(c * HIGH, (c + 1) * HIGH)
    k = max(c - 2, 0)
    gain = (j0[rows, :] + j2[rows, :]) + (j1[rows, :] + j3[rows, :])
    return vel[rows, :] + prop[k * HIGH : (k + 1) * HIGH, :] * gain


def gather_kernel(meta, vel, prop, j0, j1, j2, j3, x, idx, vel_out, u_out, share, words):
    rows = [moved(vel, prop, j0, j1, j2, j3, c) for c in range(6)]
    for c in range(6):
        vel_out[c * HIGH : (c + 1) * HIGH, :] = rows[c]
    unit = fixed_words(rows, words)

    def two_groups(pair, _):
        project([pair * 2, pair * 2 + 1], words, unit, x, idx, u_out, True)
        return 0

    lax.fori_loop(0, (meta[COUNT] + 1) >> 1, two_groups, 0)

    def one_share(q, _):
        share[q, 0] = u_out[pl.ds(meta[q], 8), :]
        share[q, 1] = u_out[pl.ds(meta[PEERS + q], 8), :]
        return 0

    lax.fori_loop(0, PEERS, one_share, 0)


def final_kernel(vel, prop, j0, j1, j2, j3, out):
    for c in range(6):
        rows = moved(vel, prop, j0, j1, j2, j3, c)
        for h in range(HIGH):
            out[c : c + 1, h * LANES : (h + 1) * LANES] = rows[h : h + 1]


def unpack_kernel(live, meta, imp, warm, out):
    lanes = lax.broadcasted_iota(jnp.int32, (1, LANES), 1)

    def one_partner(q, _):
        offset = jnp.int32(0)
        for b in range(BLK):
            count = live[q * BLK + b]
            shift = offset & (LANES - 1)
            row = meta[q] + (offset >> 7)
            here = imp[pl.ds(row, 1), :]
            after = imp[pl.ds(row + 1, 1), :]
            both = jnp.where(lanes >= shift, here, after)
            back = pltpu.roll(both, (LANES - shift) & (LANES - 1), 1)
            slot = pl.ds(q * BLK + b, 1)
            out[slot, :] = jnp.where(lanes < count, back, warm[slot, :])
            offset = offset + count
        return 0

    lax.fori_loop(0, PEERS, one_partner, 0, unroll=2)


def shape(*dims, dtype=F32):
    return jax.ShapeDtypeStruct(dims, dtype)


def call(kernel, ins, outs, scratch=(), name=None):
    return pl.pallas_call(
        kernel,
        in_specs=list(ins),
        out_specs=tuple(SMEM if o.dtype == jnp.int32 and len(o.shape) == 1 else VMEM for o in outs),
        out_shape=tuple(outs),
        scratch_shapes=list(scratch),
        compiler_params=pltpu.CompilerParams(vmem_limit_bytes=16 << 20),
        cost_estimate=pl.CostEstimate(
            flops=10_000_000, bytes_accessed=4_000_000, transcendentals=0
        ),
        name=name,
    )


def pack(live, geometry, first, second, target, warm):
    rows = pl.BlockSpec((PART * BLK, LANES), lambda i: (i, 0))
    out = pl.BlockSpec((PART, 64, LANES), lambda i: (i, 0, 0))
    return pl.pallas_call(
        pack_kernel,
        grid=(PEERS // PART,),
        in_specs=[SMEM, pl.BlockSpec((9, PART * BLK * LANES), lambda i: (0, i))] + [rows] * 4,
        out_specs=(out, out),
        out_shape=(shape(PEERS, 64, LANES),) * 2,
        scratch_shapes=[pltpu.VMEM((64, LANES), F32)] * 2 + [pltpu.VMEM((16, 8, LANES), F32)] * 4,
        compiler_params=pltpu.CompilerParams(
            dimension_semantics=("arbitrary",), vmem_limit_bytes=60 << 20
        ),
        name="pack",
    )(live, geometry, first, second, target, warm)


def on_device(
    velocity, properties, first_body, second_body, geometry, target_speed, warm_impulse, live_pairs
):
    table = lambda array: array.reshape(ROWS, LANES)
    warm = table(warm_impulse)
    words = pltpu.VMEM((64, LANES), jnp.int32)

    def streams(groups, terms, length):
        stream = shape(length, LANES)
        return [
            shape(groups, terms, 8, LANES), shape(length, LANES, dtype=jnp.int32), stream, stream, stream
        ]

    send, local = pack(
        live_pairs, geometry, table(first_body), table(second_body), table(target_speed), warm
    )
    received = lax.all_to_all(send, "owner", split_axis=0, concat_axis=0, tiled=True)
    *side_a, meta_a, share, vel, prop = call(
        first_kernel,
        [SMEM] + [VMEM] * 4,
        streams(ROWS // 8, 7, STAGE)
        + [
            shape(PEERS + 1, dtype=jnp.int32), shape(PEERS, 2, 8, LANES),
            shape(96, LANES), shape(64, LANES),
        ],
        [pltpu.VMEM((STAGE * 8, LANES), F32)] * 2 + [words],
        name="first",
    )(live_pairs, send, local, velocity, properties)
    *side_b, meta_b, share = call(
        second_kernel,
        [VMEM] * 4,
        streams(ROWS // 8, 6, STAGE)
        + [shape(PEERS + 1, dtype=jnp.int32), shape(PEERS, 4, 8, LANES)],
        [pltpu.VMEM((STAGE * 8, LANES), F32), words, pltpu.SMEM((PEERS,), jnp.int32)],
        name="second",
    )(received, share, vel, prop)
    n_sub = lax.axis_size("sub")
    stream = shape(STREAM, LANES)
    scratch = pltpu.VMEM((STREAM, LANES), F32)
    for iteration in range(ITERS):
        told = lax.all_to_all(share, "owner", split_axis=0, concat_axis=0, tiled=True)
        if iteration == 0:
            own, imp, weight, x, idx, meta = call(
                functools.partial(apply_kernel, True),
                [SMEM] * 2 + [VMEM] * 11,
                [shape(96, LANES), stream, stream]
                + streams(GROUPS, 7, STREAM)[:2]
                + [shape(COUNT + 1, dtype=jnp.int32)],
                [scratch] * 5,
                name="apply",
            )(meta_a, meta_b, *side_a, *side_b, told)
        else:
            own, imp = call(
                functools.partial(apply_kernel, False),
                [SMEM] + [VMEM] * 6,
                [shape(96, LANES), stream],
                [scratch],
                name="apply",
            )(meta, x, idx, imp, u, weight, told)
        gains = [own] + [
            lax.ppermute(own, "sub", [(i, (i + d) % n_sub) for i in range(n_sub)])
            for d in (1, 2, 3)
        ]
        if iteration < ITERS - 1:
            vel, u, share = call(
                gather_kernel,
                [SMEM] + [VMEM] * 8,
                [shape(96, LANES), stream, shape(PEERS, 2, 8, LANES)],
                [words],
                name="gather",
            )(meta, vel, prop, *gains, x, idx)
    (impulse,) = call(
        unpack_kernel, [SMEM, SMEM, VMEM, VMEM], [shape(ROWS, LANES)], name="unpack"
    )(live_pairs, meta, imp, warm)
    (out,) = call(final_kernel, [VMEM] * 6, [shape(6, HIGH * LANES)], name="final")(
        vel, prop, *gains
    )
    return (out, impulse.reshape(-1))


def solution(mesh):
    return jax.shard_map(
        on_device,
        mesh=mesh,
        in_specs=(
            P(None, "owner"),
            P(None, "owner"),
            P(("owner", "sub")),
            P(("owner", "sub")),
            P(None, ("owner", "sub")),
            P(("owner", "sub")),
            P(("owner", "sub")),
            P(("owner", "sub")),
        ),
        out_specs=(P(None, "owner"), P(("owner", "sub"))),
        check_vma=False,
    )
```

```python
import functools

import jax
import jax.numpy as jnp
from jax import lax
from jax.experimental import pallas as pl
from jax.experimental.pallas import tpu as pltpu
from jax.sharding import PartitionSpec as P

ITERS = 4
relax = 0.1
F32 = jnp.float32
BF16 = jnp.bfloat16
LANES = 128
BLK = 8
PEERS = 32
HIGH = 16
ROWS = PEERS * BLK
STAGE = ROWS + 2 * BLK
HALF = float(1 << 20)
CHUNK = 6
GROUPS = 2 * ROWS // 8 + CHUNK
STREAM = GROUPS * 8
COUNT = 2 * PEERS
PART = 8
WAYS = 4
VMEM = pl.BlockSpec(memory_space=pltpu.VMEM)
SMEM = pl.BlockSpec(memory_space=pltpu.SMEM)


def lane_iota():
    return lax.broadcasted_iota(jnp.int32, (8, LANES), 1)


def row_iota():
    return lax.broadcasted_iota(jnp.int32, (8, LANES), 0)


def pack_kernel(sent, live, geom, index, value, out, *scratch):
    start = pl.program_id(0) * PART
    lanes = lane_iota()
    subs = row_iota()
    fill = jnp.where((subs == 4) & sent, -1.0, 0.0).astype(F32)
    mixes = (subs >= 3) & (subs < 6) if sent else subs >= 6

    def one_partner(q, mixed, packed):
        rows = pl.ds(pl.multiple_of(q * BLK, BLK), BLK)
        mixed[pl.ds(4 if sent else 7, 8, stride=8), :] = (index[rows, :] & (HIGH * LANES - 1)).astype(F32)
        mixed[pl.ds(5 if sent else 6, 8, stride=8), :] = value[rows, :]
        cols = [pl.ds(pl.multiple_of(q * BLK * LANES + b * LANES, LANES), LANES) for b in range(BLK)]
        if sent:
            for b in range(BLK):
                mixed[pl.ds(8 * b + 3, 1), :] = geom[8:9, cols[b]]
        offset = jnp.int32(0)
        current = jnp.zeros((8, LANES), F32)
        for b in range(BLK):
            shift = offset & (LANES - 1)
            row = offset >> 7
            both = jnp.where(mixes, mixed[8 * b : 8 * b + 8, :], geom[0:8, cols[b]])
            rolled = pltpu.roll(both, shift, 1)
            current = jnp.where(lanes < shift, current, rolled)
            packed[row] = current
            offset = offset + live[(start + q) * BLK + b]
            spill = jnp.broadcast_to((offset >> 7) > row, (8, LANES))
            current = jnp.where(spill, rolled, current)
        packed[offset >> 7] = current
        for r in range(BLK):
            out[q, 8 * r : 8 * r + 8, :] = jnp.where(lanes + r * LANES < offset, packed[r], fill)

    def some_partners(step, _):
        for k in range(WAYS):
            one_partner(step * WAYS + k, *scratch[2 * k : 2 * k + 2])
        return 0

    lax.fori_loop(0, PART // WAYS, some_partners, 0)


def gather_rows(tables, index, count):
    lows = [i & (LANES - 1) for i in index]
    highs = [i >> 7 for i in index]
    found = [[None] * count for _ in index]
    for h in range(HIGH):
        masks = [hi == h for hi in highs]
        for c in range(count):
            ref, start = tables[c]
            line = jnp.broadcast_to(ref[start + h : start + h + 1, :], (8, LANES))
            for k in range(len(index)):
                got = jnp.take_along_axis(line, lows[k], axis=1, mode="promise_in_bounds")
                found[k][c] = got if h == 0 else jnp.where(masks[k], got, found[k][c])
    return found


def group_rows(g):
    return pl.ds(pl.multiple_of(g * 8, 8), 8)


def fixed_words(rows, words):
    most = jnp.abs(rows[0])
    for part in rows[1:]:
        most = jnp.maximum(most, jnp.abs(part))
    most = jnp.max(jnp.max(most, axis=0, keepdims=True), axis=1, keepdims=True)
    most = jnp.maximum(jnp.broadcast_to(most, (HIGH, LANES)), 1e-30)
    scale = (HALF - 2.0) / most
    whole = [(part * scale + (HALF + 0.5)).astype(jnp.int32) for part in rows]
    for k in range(4):
        extra = whole[4 + k // 2]
        extra = extra >> 11 if k % 2 else extra & 2047
        words[k * HIGH : (k + 1) * HIGH, :] = whole[k] | (extra << 21)
    return most[0:8] * (1.0 / (HALF - 2.0))


def project(groups, words, unit, x, idx, u_out, offset):
    rows = [group_rows(g) for g in groups]
    got = gather_rows([(words, HIGH * k) for k in range(4)], [idx[r, :] for r in rows], 4)
    for k, g in enumerate(groups):
        tops = [lax.shift_right_logical(w, 21) for w in got[k]]
        whole = [w & ((1 << 21) - 1) for w in got[k]]
        whole += [tops[0] | (tops[1] << 11), tops[2] | (tops[3] << 11)]
        u = jnp.zeros((8, LANES), F32)
        for c in range(6):
            u = u + x[g, c] * (whole[c] - (1 << 20)).astype(F32)
        u = u * unit
        u_out[rows[k], :] = u - x[g, 6] if offset else u


def prepare(first, total, d0, d1, vel, prop, words, x_out, idx_out, imp_out, u_out, m_out):
    unit = fixed_words([vel[c * HIGH : (c + 1) * HIGH, :] for c in range(6)], words)

    def load(g):
        base = g * 64

        def get(ref, k):
            return ref[pl.ds(base + k, 8, stride=8), :]

        flag = get(d0, 4)
        alive = (flag >= 0.0) & (row_iota() + g * 8 < total)
        source, arms, index = (d1, (3, 4, 5), get(d1, 7)) if first else (d0, (6, 7, 3), flag)
        normal = [get(source, k) for k in (0, 1, 2)]
        arm = [get(source, k) for k in arms]
        cross = [
            arm[1] * normal[2] - arm[2] * normal[1],
            arm[2] * normal[0] - arm[0] * normal[2],
            arm[0] * normal[1] - arm[1] * normal[0],
        ]
        return get, alive, jnp.where(alive, index, 0.0).astype(jnp.int32), normal, cross

    def two_groups(pair, _):
        groups = [pair * 2, pair * 2 + 1]
        indices = [load(g)[2] for g in groups]
        masses = gather_rows([(prop, HIGH * c) for c in range(4)], indices, 4)
        for k, g in enumerate(groups):
            get, alive, index, normal, cross = load(g)
            mass = masses[k][0]
            for c in range(3):
                mass = mass + cross[c] * cross[c] * masses[k][1 + c]
            rows = group_rows(g)
            m_out[rows, :] = jnp.where(alive, mass, -1.0)
            idx_out[rows, :] = index
            imp_out[rows, :] = jnp.where(alive, get(d0, 5), 0.0)
            sign = 1.0 if first else -1.0
            for c, term in enumerate(normal + cross):
                x_out[g, c] = jnp.where(alive, sign * term, 0.0)
            if first:
                x_out[g, 6] = jnp.where(alive, get(d1, 6), 0.0)
        project(groups, words, unit, x_out, idx_out, u_out, first)
        return 0

    lax.fori_loop(0, (total + 15) >> 4, two_groups, 0)


def first_kernel(
    live, send, local, velocity, properties,
    x_out, idx_out, imp_out, u_out, m_out, meta, share, vel, prop, d0, d1, words,
):
    for c in range(6):
        for h in range(HIGH):
            vel[c * HIGH + h : c * HIGH + h + 1, :] = velocity[c : c + 1, h * LANES : (h + 1) * LANES]
    for c in range(4):
        for h in range(HIGH):
            prop[c * HIGH + h : c * HIGH + h + 1, :] = properties[c : c + 1, h * LANES : (h + 1) * LANES]

    def one_partner(q, base):
        count = live[q * BLK]
        for b in range(1, BLK):
            count = count + live[q * BLK + b]
        meta[q] = base
        rows = pl.ds(pl.multiple_of(base * 8, 8), 64)
        d0[rows, :] = send[q]
        d1[rows, :] = local[q]
        return base + ((count + LANES - 1) >> 7)

    total = lax.fori_loop(0, PEERS, one_partner, jnp.int32(0), unroll=4)
    meta[PEERS] = total
    prepare(True, total, d0, d1, vel, prop, words, x_out, idx_out, imp_out, u_out, m_out)

    def one_share(q, _):
        rows = pl.ds(meta[q], 8)
        share[q, 0] = u_out[rows, :]
        share[q, 1] = m_out[rows, :]
        return 0

    lax.fori_loop(0, PEERS, one_share, 0, unroll=8)


def second_kernel(
    received, share_first, vel, prop,
    x_out, idx_out, imp_out, u_out, m_out, meta, share, d0, words, used, sem,
):
    copy = pltpu.make_async_copy(share_first, share.at[:, 0:2], sem)
    copy.start()

    def count_rows(q, _):
        flags = received[q, pl.ds(4, 8, stride=8), :]
        used[q] = jnp.max(jnp.where(flags >= 0.0, row_iota() + 1, 0))
        return 0

    lax.fori_loop(0, PEERS, count_rows, 0, unroll=8)

    def one_partner(q, base):
        meta[q] = base
        d0[pl.ds(pl.multiple_of(base * 8, 8), 64), :] = received[q]
        return base + used[q]

    total = lax.fori_loop(0, PEERS, one_partner, jnp.int32(0), unroll=4)
    meta[PEERS] = total
    prepare(False, total, d0, None, vel, prop, words, x_out, idx_out, imp_out, u_out, m_out)

    def one_share(q, _):
        rows = pl.ds(meta[q], 8)
        share[q, 2] = u_out[rows, :]
        share[q, 3] = m_out[rows, :]
        return 0

    lax.fori_loop(0, PEERS, one_share, 0, unroll=8)
    copy.wait()


def merge(side, shift, meta_in, ins, outs):
    terms = 6 if side else 7

    def one_group(g, _):
        for c in range(7):
            outs[0][g + shift, c] = ins[0][g, c] if c < terms else jnp.zeros((8, LANES), F32)
        for k in range(1, 5):
            outs[k][group_rows(g + shift), :] = ins[k][group_rows(g), :]
        return 0

    count = (meta_in[PEERS] + 7) >> 3
    lax.fori_loop(0, count, one_group, 0)
    return shift + count


def apply_kernel(start, *refs):
    if start:
        meta_a, meta_b = refs[:2]
        sides = refs[2:7], refs[7:12]
        received, j_out, new, weight, x, idx, meta, imp, u, w, other, mass = refs[12:]
        shift = merge(0, 0, meta_a, sides[0], (x, idx, imp, u, w))
        groups = merge(1, shift, meta_b, sides[1], (x, idx, imp, u, w))
        meta[COUNT] = groups
        zero = jnp.zeros((8, LANES), F32)
        for k in range(CHUNK):
            rows = group_rows(groups + k)
            for c in range(7):
                x[groups + k, c] = zero
            idx[rows, :] = zero.astype(jnp.int32)
            imp[rows, :] = zero
            u[rows, :] = zero
            w[rows, :] = zero - 1.0
    else:
        meta, x, idx, imp, u, weight, received, j_out, new, other = refs
    step = 2 if start else 1

    def one_partner(p, _):
        if start:
            meta[p] = meta_a[p]
            mass[pl.ds(meta[p], 8), :] = received[p, 3]
        other[pl.ds(meta[p], 8), :] = received[p, step]
        return 0

    def second_partner(p, _):
        if start:
            meta[PEERS + p] = meta_b[p] + shift * 8
            mass[pl.ds(meta[PEERS + p], 8), :] = received[p, 1]
        other[pl.ds(meta[PEERS + p], 8), :] = received[p, 0]
        return 0

    lax.fori_loop(0, PEERS, one_partner, 0, unroll=8)
    lax.fori_loop(0, PEERS, second_partner, 0, unroll=8)
    iota_high = lax.broadcasted_iota(jnp.int32, (HIGH, LANES), 0)
    iota_low = lax.broadcasted_iota(jnp.int32, (LANES, LANES), 0)

    def one_chunk(i, total):
        lefts = []
        rights = []
        for j in range(CHUNK):
            g = i * CHUNK + j
            rows = group_rows(g)
            if start:
                mine = w[rows, :]
                alive = mine > 0.0
                scale = jnp.where(alive, relax / (mine + mass[rows, :]), 0.0)
                weight[rows, :] = scale
            else:
                scale = weight[rows, :]
                alive = scale > 0.0
            before = imp[rows, :]
            fresh = jnp.maximum(before - (u[rows, :] + other[rows, :]) * scale, 0.0)
            fresh = jnp.where(alive, fresh, before)
            applied = fresh - before
            new[rows, :] = fresh
            values = [applied * x[g, c] for c in range(6)]
            tops = [v.astype(BF16).astype(F32) for v in values]
            pieces = tops + [v - t for v, t in zip(values, tops)]
            index = idx[rows, :]
            low = index & (LANES - 1)
            high = index >> 7
            for b in range(8):
                mask = jnp.broadcast_to(high[b : b + 1], (HIGH, LANES)) == iota_high
                lefts.append(
                    jnp.concatenate(
                        [
                            jnp.where(mask, jnp.broadcast_to(v[b : b + 1], (HIGH, LANES)), 0.0).astype(BF16)
                            for v in pieces
                        ],
                        axis=0,
                    )
                )
                hit = jnp.broadcast_to(low[b : b + 1], (LANES, LANES)) == iota_low
                rights.append(jnp.where(hit, 1.0, 0.0).astype(BF16))
        return total + lax.dot_general(
            jnp.concatenate(lefts, axis=1),
            jnp.concatenate(rights, axis=1),
            (((1,), (1,)), ((), ())),
            preferred_element_type=F32,
        )

    chunks = (meta[COUNT] + CHUNK - 1) // CHUNK
    total = lax.fori_loop(0, chunks, one_chunk, jnp.zeros((12 * HIGH, LANES), F32))
    j_out[...] = total[0:96] + total[96:192]


def moved(vel, prop, j0, j1, j2, j3, c):
    rows = slice(c * HIGH, (c + 1) * HIGH)
    k = max(c - 2, 0)
    gain = (j0[rows, :] + j2[rows, :]) + (j1[rows, :] + j3[rows, :])
    return vel[rows, :] + prop[k * HIGH : (k + 1) * HIGH, :] * gain


def gather_kernel(meta, vel, prop, j0, j1, j2, j3, x, idx, vel_out, u_out, share, words):
    rows = [moved(vel, prop, j0, j1, j2, j3, c) for c in range(6)]
    for c in range(6):
        vel_out[c * HIGH : (c + 1) * HIGH, :] = rows[c]
    unit = fixed_words(rows, words)

    def two_groups(pair, _):
        project([pair * 2, pair * 2 + 1], words, unit, x, idx, u_out, True)
        return 0

    lax.fori_loop(0, (meta[COUNT] + 1) >> 1, two_groups, 0)

    def one_share(q, _):
        share[q, 0] = u_out[pl.ds(meta[q], 8), :]
        share[q, 1] = u_out[pl.ds(meta[PEERS + q], 8), :]
        return 0

    lax.fori_loop(0, PEERS, one_share, 0, unroll=8)


def final_kernel(vel, prop, j0, j1, j2, j3, out):
    for c in range(6):
        rows = moved(vel, prop, j0, j1, j2, j3, c)
        for h in range(HIGH):
            out[c : c + 1, h * LANES : (h + 1) * LANES] = rows[h : h + 1]


def unpack_kernel(live, meta, imp, warm, out):
    lanes = lax.broadcasted_iota(jnp.int32, (1, LANES), 1)

    def one_partner(q, _):
        offset = jnp.int32(0)
        for b in range(BLK):
            count = live[q * BLK + b]
            shift = offset & (LANES - 1)
            row = meta[q] + (offset >> 7)
            here = imp[pl.ds(row, 1), :]
            after = imp[pl.ds(row + 1, 1), :]
            both = jnp.where(lanes >= shift, here, after)
            back = pltpu.roll(both, (LANES - shift) & (LANES - 1), 1)
            slot = pl.ds(q * BLK + b, 1)
            out[slot, :] = jnp.where(lanes < count, back, warm[slot, :])
            offset = offset + count
        return 0

    lax.fori_loop(0, PEERS, one_partner, 0, unroll=4)


def shape(*dims, dtype=F32):
    return jax.ShapeDtypeStruct(dims, dtype)


def call(kernel, ins, outs, scratch=(), name=None):
    return pl.pallas_call(
        kernel,
        in_specs=list(ins),
        out_specs=tuple(SMEM if o.dtype == jnp.int32 and len(o.shape) == 1 else VMEM for o in outs),
        out_shape=tuple(outs),
        scratch_shapes=list(scratch),
        compiler_params=pltpu.CompilerParams(vmem_limit_bytes=16 << 20),
        cost_estimate=pl.CostEstimate(
            flops=10_000_000, bytes_accessed=4_000_000, transcendentals=0
        ),
        name=name,
    )


def pack(sent, live, geometry, index, value):
    rows = pl.BlockSpec((PART * BLK, LANES), lambda i: (i, 0))
    return pl.pallas_call(
        functools.partial(pack_kernel, sent),
        grid=(PEERS // PART,),
        in_specs=[SMEM, pl.BlockSpec((9, PART * BLK * LANES), lambda i: (0, i)), rows, rows],
        out_specs=pl.BlockSpec((PART, 64, LANES), lambda i: (i, 0, 0)),
        out_shape=shape(PEERS, 64, LANES),
        scratch_shapes=[pltpu.VMEM((64, LANES), F32), pltpu.VMEM((16, 8, LANES), F32)] * WAYS,
        compiler_params=pltpu.CompilerParams(
            dimension_semantics=("arbitrary",), vmem_limit_bytes=(60 if sent else 16) << 20
        ),
        cost_estimate=pl.CostEstimate(
            flops=10_000_000, bytes_accessed=4_000_000, transcendentals=0
        ),
        name="pack_sent" if sent else "pack_local",
    )(live, geometry, index, value)


def on_device(
    velocity, properties, first_body, second_body, geometry, target_speed, warm_impulse, live_pairs
):
    table = lambda array: array.reshape(ROWS, LANES)
    warm = table(warm_impulse)
    words = pltpu.VMEM((64, LANES), jnp.int32)

    def streams(groups, terms, length):
        stream = shape(length, LANES)
        return [
            shape(groups, terms, 8, LANES), shape(length, LANES, dtype=jnp.int32), stream, stream, stream
        ]

    send = pack(True, live_pairs, geometry, table(second_body), warm)
    local = pack(False, live_pairs, geometry, table(first_body), table(target_speed))
    received = lax.all_to_all(send, "owner", split_axis=0, concat_axis=0, tiled=True)
    *side_a, meta_a, share, vel, prop = call(
        first_kernel,
        [SMEM] + [VMEM] * 4,
        streams(ROWS // 8, 7, STAGE)
        + [
            shape(PEERS + 1, dtype=jnp.int32), shape(PEERS, 2, 8, LANES),
            shape(96, LANES), shape(64, LANES),
        ],
        [pltpu.VMEM((STAGE * 8, LANES), F32)] * 2 + [words],
        name="first",
    )(live_pairs, send, local, velocity, properties)
    *side_b, meta_b, share = call(
        second_kernel,
        [VMEM, pl.BlockSpec(memory_space=pltpu.HBM), VMEM, VMEM],
        streams(ROWS // 8, 6, STAGE)
        + [shape(PEERS + 1, dtype=jnp.int32), shape(PEERS, 4, 8, LANES)],
        [pltpu.VMEM((STAGE * 8, LANES), F32), words, pltpu.SMEM((PEERS,), jnp.int32), pltpu.SemaphoreType.DMA],
        name="second",
    )(received, share, vel, prop)
    n_sub = lax.axis_size("sub")
    stream = shape(STREAM, LANES)
    scratch = pltpu.VMEM((STREAM, LANES), F32)
    for iteration in range(ITERS):
        told = lax.all_to_all(share, "owner", split_axis=0, concat_axis=0, tiled=True)
        if iteration == 0:
            own, imp, weight, x, idx, meta = call(
                functools.partial(apply_kernel, True),
                [SMEM] * 2 + [VMEM] * 11,
                [shape(96, LANES), stream, stream]
                + streams(GROUPS, 7, STREAM)[:2]
                + [shape(COUNT + 1, dtype=jnp.int32)],
                [scratch] * 5,
                name="apply",
            )(meta_a, meta_b, *side_a, *side_b, told)
        else:
            own, imp = call(
                functools.partial(apply_kernel, False),
                [SMEM] + [VMEM] * 6,
                [shape(96, LANES), stream],
                [scratch],
                name="apply",
            )(meta, x, idx, imp, u, weight, told)
        gains = [own] + [
            lax.ppermute(own, "sub", [(i, (i + d) % n_sub) for i in range(n_sub)])
            for d in (1, 2, 3)
        ]
        if iteration < ITERS - 1:
            vel, u, share = call(
                gather_kernel,
                [SMEM] + [VMEM] * 8,
                [shape(96, LANES), stream, shape(PEERS, 2, 8, LANES)],
                [words],
                name="gather",
            )(meta, vel, prop, *gains, x, idx)
    (impulse,) = call(
        unpack_kernel, [SMEM, SMEM, VMEM, VMEM], [shape(ROWS, LANES)], name="unpack"
    )(live_pairs, meta, imp, warm)
    (out,) = call(final_kernel, [VMEM] * 6, [shape(6, HIGH * LANES)], name="final")(
        vel, prop, *gains
    )
    return (out, impulse.reshape(-1))


def solution(mesh):
    return jax.shard_map(
        on_device,
        mesh=mesh,
        in_specs=(
            P(None, "owner"),
            P(None, "owner"),
            P(("owner", "sub")),
            P(("owner", "sub")),
            P(None, ("owner", "sub")),
            P(("owner", "sub")),
            P(("owner", "sub")),
            P(("owner", "sub")),
        ),
        out_specs=(P(None, "owner"), P(("owner", "sub"))),
        check_vma=False,
    )
```

```python
import functools

import jax
import jax.numpy as jnp
from jax import lax
from jax.experimental import pallas as pl
from jax.experimental.pallas import tpu as pltpu
from jax.sharding import PartitionSpec as P

ITERS = 4
relax = 0.1
F32 = jnp.float32
BF16 = jnp.bfloat16
LANES = 128
BLK = 8
PEERS = 32
HIGH = 16
ROWS = PEERS * BLK
STAGE = ROWS + 2 * BLK
HALF = float(1 << 20)
CHUNK = 5
GROUPS = 2 * ROWS // 8 + CHUNK
STREAM = GROUPS * 8
COUNT = 2 * PEERS
PART = 16
WAYS = 4
VMEM = pl.BlockSpec(memory_space=pltpu.VMEM)
SMEM = pl.BlockSpec(memory_space=pltpu.SMEM)


def lane_iota():
    return lax.broadcasted_iota(jnp.int32, (8, LANES), 1)


def row_iota():
    return lax.broadcasted_iota(jnp.int32, (8, LANES), 0)


def pack_kernel(sent, live, geom, index, value, out, *scratch):
    start = pl.program_id(0) * PART
    lanes = lane_iota()
    subs = row_iota()
    fill = jnp.where((subs == 4) & sent, -1.0, 0.0).astype(F32)
    mixes = (subs >= 3) & (subs < 6) if sent else subs >= 6

    def one_partner(q, mixed, packed):
        rows = pl.ds(pl.multiple_of(q * BLK, BLK), BLK)
        mixed[pl.ds(4 if sent else 7, 8, stride=8), :] = (index[rows, :] & (HIGH * LANES - 1)).astype(F32)
        mixed[pl.ds(5 if sent else 6, 8, stride=8), :] = value[rows, :]
        cols = [pl.ds(pl.multiple_of(q * BLK * LANES + b * LANES, LANES), LANES) for b in range(BLK)]
        if sent:
            for b in range(BLK):
                mixed[pl.ds(8 * b + 3, 1), :] = geom[8:9, cols[b]]
        offset = jnp.int32(0)
        current = jnp.zeros((8, LANES), F32)
        for b in range(BLK):
            shift = offset & (LANES - 1)
            row = offset >> 7
            both = jnp.where(mixes, mixed[8 * b : 8 * b + 8, :], geom[0:8, cols[b]])
            rolled = pltpu.roll(both, shift, 1)
            current = jnp.where(lanes < shift, current, rolled)
            packed[row] = current
            offset = offset + live[(start + q) * BLK + b]
            spill = jnp.broadcast_to((offset >> 7) > row, (8, LANES))
            current = jnp.where(spill, rolled, current)
        packed[offset >> 7] = current
        for r in range(BLK):
            out[q, 8 * r : 8 * r + 8, :] = jnp.where(lanes + r * LANES < offset, packed[r], fill)

    def some_partners(step, _):
        for k in range(WAYS):
            one_partner(step * WAYS + k, *scratch[2 * k : 2 * k + 2])
        return 0

    lax.fori_loop(0, PART // WAYS, some_partners, 0)


def gather_rows(tables, index, count):
    lows = [i & (LANES - 1) for i in index]
    highs = [i >> 7 for i in index]
    found = [[None] * count for _ in index]
    for h in range(HIGH):
        masks = [hi == h for hi in highs]
        for c in range(count):
            ref, start = tables[c]
            line = jnp.broadcast_to(ref[start + h : start + h + 1, :], (8, LANES))
            for k in range(len(index)):
                got = jnp.take_along_axis(line, lows[k], axis=1, mode="promise_in_bounds")
                found[k][c] = got if h == 0 else jnp.where(masks[k], got, found[k][c])
    return found


def group_rows(g):
    return pl.ds(pl.multiple_of(g * 8, 8), 8)


def fixed_words(rows, words):
    most = jnp.abs(rows[0])
    for part in rows[1:]:
        most = jnp.maximum(most, jnp.abs(part))
    most = jnp.max(jnp.max(most, axis=0, keepdims=True), axis=1, keepdims=True)
    most = jnp.maximum(jnp.broadcast_to(most, (HIGH, LANES)), 1e-30)
    scale = (HALF - 2.0) / most
    whole = [(part * scale + (HALF + 0.5)).astype(jnp.int32) for part in rows]
    for k in range(4):
        extra = whole[4 + k // 2]
        extra = extra >> 11 if k % 2 else extra & 2047
        words[k * HIGH : (k + 1) * HIGH, :] = whole[k] | (extra << 21)
    return most[0:8] * (1.0 / (HALF - 2.0))


def project(groups, words, unit, x, idx, u_out, offset):
    rows = [group_rows(g) for g in groups]
    got = gather_rows([(words, HIGH * k) for k in range(4)], [idx[r, :] for r in rows], 4)
    for k, g in enumerate(groups):
        tops = [lax.shift_right_logical(w, 21) for w in got[k]]
        whole = [w & ((1 << 21) - 1) for w in got[k]]
        whole += [tops[0] | (tops[1] << 11), tops[2] | (tops[3] << 11)]
        u = jnp.zeros((8, LANES), F32)
        for c in range(6):
            u = u + x[g, c] * (whole[c] - (1 << 20)).astype(F32)
        u = u * unit
        u_out[rows[k], :] = u - x[g, 6] if offset else u


def prepare(first, total, d0, d1, vel, prop, words, x_out, idx_out, imp_out, u_out, m_out):
    unit = fixed_words([vel[c * HIGH : (c + 1) * HIGH, :] for c in range(6)], words)

    def load(g):
        base = g * 64

        def get(ref, k):
            return ref[pl.ds(base + k, 8, stride=8), :]

        flag = get(d0, 4)
        alive = (flag >= 0.0) & (row_iota() + g * 8 < total)
        source, arms, index = (d1, (3, 4, 5), get(d1, 7)) if first else (d0, (6, 7, 3), flag)
        normal = [get(source, k) for k in (0, 1, 2)]
        arm = [get(source, k) for k in arms]
        cross = [
            arm[1] * normal[2] - arm[2] * normal[1],
            arm[2] * normal[0] - arm[0] * normal[2],
            arm[0] * normal[1] - arm[1] * normal[0],
        ]
        return get, alive, jnp.where(alive, index, 0.0).astype(jnp.int32), normal, cross

    def two_groups(pair, _):
        groups = [pair * 2, pair * 2 + 1]
        indices = [load(g)[2] for g in groups]
        masses = gather_rows([(prop, HIGH * c) for c in range(4)], indices, 4)
        for k, g in enumerate(groups):
            get, alive, index, normal, cross = load(g)
            mass = masses[k][0]
            for c in range(3):
                mass = mass + cross[c] * cross[c] * masses[k][1 + c]
            rows = group_rows(g)
            m_out[rows, :] = jnp.where(alive, mass, -1.0)
            idx_out[rows, :] = index
            imp_out[rows, :] = jnp.where(alive, get(d0, 5), 0.0)
            sign = 1.0 if first else -1.0
            for c, term in enumerate(normal + cross):
                x_out[g, c] = jnp.where(alive, sign * term, 0.0)
            if first:
                x_out[g, 6] = jnp.where(alive, get(d1, 6), 0.0)
        project(groups, words, unit, x_out, idx_out, u_out, first)
        return 0

    lax.fori_loop(0, (total + 15) >> 4, two_groups, 0)


def first_kernel(
    live, send, local, velocity, properties,
    x_out, idx_out, imp_out, u_out, m_out, meta, share, vel, prop, d0, d1, words,
):
    for c in range(6):
        for h in range(HIGH):
            vel[c * HIGH + h : c * HIGH + h + 1, :] = velocity[c : c + 1, h * LANES : (h + 1) * LANES]
    for c in range(4):
        for h in range(HIGH):
            prop[c * HIGH + h : c * HIGH + h + 1, :] = properties[c : c + 1, h * LANES : (h + 1) * LANES]

    def one_partner(q, base):
        count = live[q * BLK]
        for b in range(1, BLK):
            count = count + live[q * BLK + b]
        meta[q] = base
        rows = pl.ds(pl.multiple_of(base * 8, 8), 64)
        d0[rows, :] = send[q]
        d1[rows, :] = local[q]
        return base + ((count + LANES - 1) >> 7)

    total = lax.fori_loop(0, PEERS, one_partner, jnp.int32(0), unroll=4)
    meta[PEERS] = total
    prepare(True, total, d0, d1, vel, prop, words, x_out, idx_out, imp_out, u_out, m_out)

    def one_share(q, _):
        rows = pl.ds(meta[q], 8)
        share[q, 0] = u_out[rows, :]
        share[q, 1] = m_out[rows, :]
        return 0

    lax.fori_loop(0, PEERS, one_share, 0, unroll=8)


def second_kernel(
    arrived, share_first, vel, prop,
    x_out, idx_out, imp_out, u_out, m_out, meta, share, received, d0, words, used, sem, sems,
):
    piece = PEERS // 4
    pieces = []
    for k in range(4):
        part = pl.ds(k * piece, piece)
        pieces.append(pltpu.make_async_copy(arrived.at[part], received.at[part], sems.at[k]))
        pieces[k].start()
    copy = pltpu.make_async_copy(share_first, share.at[:, 0:2], sem)
    copy.start()

    def count_rows(q, _):
        flags = received[q, pl.ds(4, 8, stride=8), :]
        used[q] = jnp.max(jnp.where(flags >= 0.0, row_iota() + 1, 0))
        return 0

    for k in range(4):
        pieces[k].wait()
        lax.fori_loop(k * piece, (k + 1) * piece, count_rows, 0, unroll=8)

    def one_partner(q, base):
        meta[q] = base
        d0[pl.ds(pl.multiple_of(base * 8, 8), 64), :] = received[q]
        return base + used[q]

    total = lax.fori_loop(0, PEERS, one_partner, jnp.int32(0), unroll=4)
    meta[PEERS] = total
    prepare(False, total, d0, None, vel, prop, words, x_out, idx_out, imp_out, u_out, m_out)

    def one_share(q, _):
        rows = pl.ds(meta[q], 8)
        share[q, 2] = u_out[rows, :]
        share[q, 3] = m_out[rows, :]
        return 0

    lax.fori_loop(0, PEERS, one_share, 0, unroll=8)
    copy.wait()


def merge(side, shift, meta_in, ins, outs):
    terms = 6 if side else 7

    def one_group(g, _):
        for c in range(7):
            outs[0][g + shift, c] = ins[0][g, c] if c < terms else jnp.zeros((8, LANES), F32)
        for k in range(1, 5):
            outs[k][group_rows(g + shift), :] = ins[k][group_rows(g), :]
        return 0

    count = (meta_in[PEERS] + 7) >> 3
    lax.fori_loop(0, count, one_group, 0)
    return shift + count


def apply_kernel(start, *refs):
    if start:
        meta_a, meta_b = refs[:2]
        sides = refs[2:7], refs[7:12]
        received, j_out, new, weight, x, idx, meta, imp, u, w, other, mass = refs[12:]
        shift = merge(0, 0, meta_a, sides[0], (x, idx, imp, u, w))
        groups = merge(1, shift, meta_b, sides[1], (x, idx, imp, u, w))
        meta[COUNT] = groups
        zero = jnp.zeros((8, LANES), F32)
        for k in range(CHUNK):
            rows = group_rows(groups + k)
            for c in range(7):
                x[groups + k, c] = zero
            idx[rows, :] = zero.astype(jnp.int32)
            imp[rows, :] = zero
            u[rows, :] = zero
            w[rows, :] = zero - 1.0
    else:
        meta, x, idx, imp, u, weight, received, j_out, new, other = refs
    step = 2 if start else 1

    def one_partner(p, _):
        if start:
            meta[p] = meta_a[p]
            mass[pl.ds(meta[p], 8), :] = received[p, 3]
        other[pl.ds(meta[p], 8), :] = received[p, step]
        return 0

    def second_partner(p, _):
        if start:
            meta[PEERS + p] = meta_b[p] + shift * 8
            mass[pl.ds(meta[PEERS + p], 8), :] = received[p, 1]
        other[pl.ds(meta[PEERS + p], 8), :] = received[p, 0]
        return 0

    lax.fori_loop(0, PEERS, one_partner, 0, unroll=8)
    lax.fori_loop(0, PEERS, second_partner, 0, unroll=8)
    iota_high = lax.broadcasted_iota(jnp.int32, (HIGH, LANES), 0)
    iota_low = lax.broadcasted_iota(jnp.int32, (LANES, LANES), 0)

    def one_chunk(i, total):
        lefts = []
        rights = []
        for j in range(CHUNK):
            g = i * CHUNK + j
            rows = group_rows(g)
            if start:
                mine = w[rows, :]
                alive = mine > 0.0
                scale = jnp.where(alive, relax / (mine + mass[rows, :]), 0.0)
                weight[rows, :] = scale
            else:
                scale = weight[rows, :]
                alive = scale > 0.0
            before = imp[rows, :]
            fresh = jnp.maximum(before - (u[rows, :] + other[rows, :]) * scale, 0.0)
            fresh = jnp.where(alive, fresh, before)
            applied = fresh - before
            new[rows, :] = fresh
            values = [applied * x[g, c] for c in range(6)]
            tops = [v.astype(BF16).astype(F32) for v in values]
            pieces = tops + [v - t for v, t in zip(values, tops)]
            index = idx[rows, :]
            low = index & (LANES - 1)
            high = index >> 7
            for b in range(8):
                mask = jnp.broadcast_to(high[b : b + 1], (HIGH, LANES)) == iota_high
                lefts.append(
                    jnp.concatenate(
                        [
                            jnp.where(mask, jnp.broadcast_to(v[b : b + 1], (HIGH, LANES)), 0.0).astype(BF16)
                            for v in pieces
                        ],
                        axis=0,
                    )
                )
                hit = jnp.broadcast_to(low[b : b + 1], (LANES, LANES)) == iota_low
                rights.append(jnp.where(hit, 1.0, 0.0).astype(BF16))
        return total + lax.dot_general(
            jnp.concatenate(lefts, axis=1),
            jnp.concatenate(rights, axis=1),
            (((1,), (1,)), ((), ())),
            preferred_element_type=F32,
        )

    chunks = (meta[COUNT] + CHUNK - 1) // CHUNK
    total = lax.fori_loop(0, chunks, one_chunk, jnp.zeros((12 * HIGH, LANES), F32))
    j_out[...] = total[0:96] + total[96:192]


def moved(vel, prop, j0, j1, j2, j3, c):
    rows = slice(c * HIGH, (c + 1) * HIGH)
    k = max(c - 2, 0)
    gain = (j0[rows, :] + j2[rows, :]) + (j1[rows, :] + j3[rows, :])
    return vel[rows, :] + prop[k * HIGH : (k + 1) * HIGH, :] * gain


def gather_kernel(meta, vel, prop, j0, j1, j2, j3, x, idx, vel_out, u_out, share, words):
    rows = [moved(vel, prop, j0, j1, j2, j3, c) for c in range(6)]
    for c in range(6):
        vel_out[c * HIGH : (c + 1) * HIGH, :] = rows[c]
    unit = fixed_words(rows, words)

    def two_groups(pair, _):
        project([pair * 2, pair * 2 + 1], words, unit, x, idx, u_out, True)
        return 0

    lax.fori_loop(0, (meta[COUNT] + 1) >> 1, two_groups, 0)

    def one_share(q, _):
        share[q, 0] = u_out[pl.ds(meta[q], 8), :]
        share[q, 1] = u_out[pl.ds(meta[PEERS + q], 8), :]
        return 0

    lax.fori_loop(0, PEERS, one_share, 0, unroll=8)


def final_kernel(vel, prop, j0, j1, j2, j3, out):
    for c in range(6):
        rows = moved(vel, prop, j0, j1, j2, j3, c)
        for h in range(HIGH):
            out[c : c + 1, h * LANES : (h + 1) * LANES] = rows[h : h + 1]


def unpack_kernel(live, meta, imp, warm, out):
    lanes = lax.broadcasted_iota(jnp.int32, (1, LANES), 1)

    def one_partner(q, _):
        offset = jnp.int32(0)
        for b in range(BLK):
            count = live[q * BLK + b]
            shift = offset & (LANES - 1)
            row = meta[q] + (offset >> 7)
            here = imp[pl.ds(row, 1), :]
            after = imp[pl.ds(row + 1, 1), :]
            both = jnp.where(lanes >= shift, here, after)
            back = pltpu.roll(both, (LANES - shift) & (LANES - 1), 1)
            slot = pl.ds(q * BLK + b, 1)
            out[slot, :] = jnp.where(lanes < count, back, warm[slot, :])
            offset = offset + count
        return 0

    lax.fori_loop(0, PEERS, one_partner, 0, unroll=4)


def shape(*dims, dtype=F32):
    return jax.ShapeDtypeStruct(dims, dtype)


def call(kernel, ins, outs, scratch=(), name=None):
    return pl.pallas_call(
        kernel,
        in_specs=list(ins),
        out_specs=tuple(SMEM if o.dtype == jnp.int32 and len(o.shape) == 1 else VMEM for o in outs),
        out_shape=tuple(outs),
        scratch_shapes=list(scratch),
        compiler_params=pltpu.CompilerParams(vmem_limit_bytes=16 << 20),
        cost_estimate=pl.CostEstimate(
            flops=10_000_000, bytes_accessed=4_000_000, transcendentals=0
        ),
        name=name,
    )


def pack(sent, live, geometry, index, value):
    rows = pl.BlockSpec((PART * BLK, LANES), lambda i: (i, 0))
    return pl.pallas_call(
        functools.partial(pack_kernel, sent),
        grid=(PEERS // PART,),
        in_specs=[SMEM, pl.BlockSpec((9, PART * BLK * LANES), lambda i: (0, i)), rows, rows],
        out_specs=pl.BlockSpec((PART, 64, LANES), lambda i: (i, 0, 0)),
        out_shape=shape(PEERS, 64, LANES),
        scratch_shapes=[pltpu.VMEM((64, LANES), F32), pltpu.VMEM((16, 8, LANES), F32)] * WAYS,
        compiler_params=pltpu.CompilerParams(
            dimension_semantics=("arbitrary",), vmem_limit_bytes=(60 if sent else 16) << 20
        ),
        cost_estimate=pl.CostEstimate(
            flops=10_000_000, bytes_accessed=4_000_000, transcendentals=0
        ),
        name="pack_sent" if sent else "pack_local",
    )(live, geometry, index, value)


def on_device(
    velocity, properties, first_body, second_body, geometry, target_speed, warm_impulse, live_pairs
):
    table = lambda array: array.reshape(ROWS, LANES)
    warm = table(warm_impulse)
    words = pltpu.VMEM((64, LANES), jnp.int32)

    def streams(groups, terms, length):
        stream = shape(length, LANES)
        return [
            shape(groups, terms, 8, LANES), shape(length, LANES, dtype=jnp.int32), stream, stream, stream
        ]

    send = pack(True, live_pairs, geometry, table(second_body), warm)
    local = pack(False, live_pairs, geometry, table(first_body), table(target_speed))
    received = lax.all_to_all(send, "owner", split_axis=0, concat_axis=0, tiled=True)
    *side_a, meta_a, share, vel, prop = call(
        first_kernel,
        [SMEM] + [VMEM] * 4,
        streams(ROWS // 8, 7, STAGE)
        + [
            shape(PEERS + 1, dtype=jnp.int32), shape(PEERS, 2, 8, LANES),
            shape(96, LANES), shape(64, LANES),
        ],
        [pltpu.VMEM((STAGE * 8, LANES), F32)] * 2 + [words],
        name="first",
    )(live_pairs, send, local, velocity, properties)
    *side_b, meta_b, share = call(
        second_kernel,
        [pl.BlockSpec(memory_space=pltpu.HBM)] * 2 + [VMEM] * 2,
        streams(ROWS // 8, 6, STAGE)
        + [shape(PEERS + 1, dtype=jnp.int32), shape(PEERS, 4, 8, LANES)],
        [
            pltpu.VMEM((PEERS, 64, LANES), F32), pltpu.VMEM((STAGE * 8, LANES), F32), words,
            pltpu.SMEM((PEERS,), jnp.int32), pltpu.SemaphoreType.DMA, pltpu.SemaphoreType.DMA((4,)),
        ],
        name="second",
    )(received, share, vel, prop)
    n_sub = lax.axis_size("sub")
    stream = shape(STREAM, LANES)
    scratch = pltpu.VMEM((STREAM, LANES), F32)
    for iteration in range(ITERS):
        told = lax.all_to_all(share, "owner", split_axis=0, concat_axis=0, tiled=True)
        if iteration == 0:
            own, imp, weight, x, idx, meta = call(
                functools.partial(apply_kernel, True),
                [SMEM] * 2 + [VMEM] * 11,
                [shape(96, LANES), stream, stream]
                + streams(GROUPS, 7, STREAM)[:2]
                + [shape(COUNT + 1, dtype=jnp.int32)],
                [scratch] * 5,
                name="apply",
            )(meta_a, meta_b, *side_a, *side_b, told)
        else:
            own, imp = call(
                functools.partial(apply_kernel, False),
                [SMEM] + [VMEM] * 6,
                [shape(96, LANES), stream],
                [scratch],
                name="apply",
            )(meta, x, idx, imp, u, weight, told)
        gains = [own] + [
            lax.ppermute(own, "sub", [(i, (i + d) % n_sub) for i in range(n_sub)])
            for d in (1, 2, 3)
        ]
        if iteration < ITERS - 1:
            vel, u, share = call(
                gather_kernel,
                [SMEM] + [VMEM] * 8,
                [shape(96, LANES), stream, shape(PEERS, 2, 8, LANES)],
                [words],
                name="gather",
            )(meta, vel, prop, *gains, x, idx)
    (impulse,) = call(
        unpack_kernel, [SMEM, SMEM, VMEM, VMEM], [shape(ROWS, LANES)], name="unpack"
    )(live_pairs, meta, imp, warm)
    (out,) = call(final_kernel, [VMEM] * 6, [shape(6, HIGH * LANES)], name="final")(
        vel, prop, *gains
    )
    return (out, impulse.reshape(-1))


def solution(mesh):
    return jax.shard_map(
        on_device,
        mesh=mesh,
        in_specs=(
            P(None, "owner"),
            P(None, "owner"),
            P(("owner", "sub")),
            P(("owner", "sub")),
            P(None, ("owner", "sub")),
            P(("owner", "sub")),
            P(("owner", "sub")),
            P(("owner", "sub")),
        ),
        out_specs=(P(None, "owner"), P(("owner", "sub"))),
        check_vma=False,
    )
```

```python
import functools

import jax
import jax.numpy as jnp
from jax import lax
from jax.experimental import pallas as pl
from jax.experimental.pallas import tpu as pltpu
from jax.sharding import PartitionSpec as P

ITERS = 4
relax = 0.1
F32 = jnp.float32
BF16 = jnp.bfloat16
LANES = 128
BLK = 8
PEERS = 32
HIGH = 16
ROWS = PEERS * BLK
STAGE = ROWS + 2 * BLK
HALF = float(1 << 20)
CHUNK = 5
GROUPS = 2 * ROWS // 8 + CHUNK
STREAM = GROUPS * 8
COUNT = 2 * PEERS
PART = 16
WAYS = 4
VMEM = pl.BlockSpec(memory_space=pltpu.VMEM)
SMEM = pl.BlockSpec(memory_space=pltpu.SMEM)


def lane_iota():
    return lax.broadcasted_iota(jnp.int32, (8, LANES), 1)


def row_iota():
    return lax.broadcasted_iota(jnp.int32, (8, LANES), 0)


def pack_kernel(sent, live, geom, index, value, out, *scratch):
    start = pl.program_id(0) * PART
    lanes = lane_iota()
    subs = row_iota()
    fill = jnp.where((subs == 4) & sent, -1.0, 0.0).astype(F32)
    mixes = (subs >= 3) & (subs < 6) if sent else subs >= 6

    def one_partner(q, mixed, packed):
        rows = pl.ds(pl.multiple_of(q * BLK, BLK), BLK)
        mixed[pl.ds(4 if sent else 7, 8, stride=8), :] = (index[rows, :] & (HIGH * LANES - 1)).astype(F32)
        mixed[pl.ds(5 if sent else 6, 8, stride=8), :] = value[rows, :]
        cols = [pl.ds(pl.multiple_of(q * BLK * LANES + b * LANES, LANES), LANES) for b in range(BLK)]
        if sent:
            for b in range(BLK):
                mixed[pl.ds(8 * b + 3, 1), :] = geom[8:9, cols[b]]
        offset = jnp.int32(0)
        current = jnp.zeros((8, LANES), F32)
        for b in range(BLK):
            shift = offset & (LANES - 1)
            row = offset >> 7
            both = jnp.where(mixes, mixed[8 * b : 8 * b + 8, :], geom[0:8, cols[b]])
            rolled = pltpu.roll(both, shift, 1)
            current = jnp.where(lanes < shift, current, rolled)
            packed[row] = current
            offset = offset + live[(start + q) * BLK + b]
            spill = jnp.broadcast_to((offset >> 7) > row, (8, LANES))
            current = jnp.where(spill, rolled, current)
        packed[offset >> 7] = current
        for r in range(BLK):
            out[q, 8 * r : 8 * r + 8, :] = jnp.where(lanes + r * LANES < offset, packed[r], fill)

    def some_partners(step, _):
        for k in range(WAYS):
            one_partner(step * WAYS + k, *scratch[2 * k : 2 * k + 2])
        return 0

    lax.fori_loop(0, PART // WAYS, some_partners, 0)


def gather_rows(tables, index, count):
    lows = [i & (LANES - 1) for i in index]
    highs = [i >> 7 for i in index]
    found = [[None] * count for _ in index]
    for h in range(HIGH):
        masks = [hi == h for hi in highs]
        for c in range(count):
            ref, start = tables[c]
            line = jnp.broadcast_to(ref[start + h : start + h + 1, :], (8, LANES))
            for k in range(len(index)):
                got = jnp.take_along_axis(line, lows[k], axis=1, mode="promise_in_bounds")
                found[k][c] = got if h == 0 else jnp.where(masks[k], got, found[k][c])
    return found


def group_rows(g):
    return pl.ds(pl.multiple_of(g * 8, 8), 8)


def fixed_words(rows, words):
    most = jnp.abs(rows[0])
    for part in rows[1:]:
        most = jnp.maximum(most, jnp.abs(part))
    most = jnp.max(jnp.max(most, axis=0, keepdims=True), axis=1, keepdims=True)
    most = jnp.maximum(jnp.broadcast_to(most, (HIGH, LANES)), 1e-30)
    scale = (HALF - 2.0) / most
    whole = [(part * scale + (HALF + 0.5)).astype(jnp.int32) for part in rows]
    for k in range(4):
        extra = whole[4 + k // 2]
        extra = extra >> 11 if k % 2 else extra & 2047
        words[k * HIGH : (k + 1) * HIGH, :] = whole[k] | (extra << 21)
    return most[0:8] * (1.0 / (HALF - 2.0))


def project(groups, words, unit, x, idx, u_out, offset):
    rows = [group_rows(g) for g in groups]
    got = gather_rows([(words, HIGH * k) for k in range(4)], [idx[r, :] for r in rows], 4)
    for k, g in enumerate(groups):
        tops = [lax.shift_right_logical(w, 21) for w in got[k]]
        whole = [w & ((1 << 21) - 1) for w in got[k]]
        whole += [tops[0] | (tops[1] << 11), tops[2] | (tops[3] << 11)]
        u = jnp.zeros((8, LANES), F32)
        for c in range(6):
            u = u + x[g, c] * (whole[c] - (1 << 20)).astype(F32)
        u = u * unit
        u_out[rows[k], :] = u - x[g, 6] if offset else u


def prepare(first, total, d0, d1, vel, prop, words, x_out, idx_out, imp_out, u_out, m_out):
    unit = fixed_words([vel[c * HIGH : (c + 1) * HIGH, :] for c in range(6)], words)

    def load(g):
        base = g * 64

        def get(ref, k):
            return ref[pl.ds(base + k, 8, stride=8), :]

        flag = get(d0, 4)
        alive = (flag >= 0.0) & (row_iota() + g * 8 < total)
        source, arms, index = (d1, (3, 4, 5), get(d1, 7)) if first else (d0, (6, 7, 3), flag)
        normal = [get(source, k) for k in (0, 1, 2)]
        arm = [get(source, k) for k in arms]
        cross = [
            arm[1] * normal[2] - arm[2] * normal[1],
            arm[2] * normal[0] - arm[0] * normal[2],
            arm[0] * normal[1] - arm[1] * normal[0],
        ]
        return get, alive, jnp.where(alive, index, 0.0).astype(jnp.int32), normal, cross

    def two_groups(pair, _):
        groups = [pair * 2, pair * 2 + 1]
        indices = [load(g)[2] for g in groups]
        masses = gather_rows([(prop, HIGH * c) for c in range(4)], indices, 4)
        for k, g in enumerate(groups):
            get, alive, index, normal, cross = load(g)
            mass = masses[k][0]
            for c in range(3):
                mass = mass + cross[c] * cross[c] * masses[k][1 + c]
            rows = group_rows(g)
            m_out[rows, :] = jnp.where(alive, mass, -1.0)
            idx_out[rows, :] = index
            imp_out[rows, :] = jnp.where(alive, get(d0, 5), 0.0)
            sign = 1.0 if first else -1.0
            for c, term in enumerate(normal + cross):
                x_out[g, c] = jnp.where(alive, sign * term, 0.0)
            if first:
                x_out[g, 6] = jnp.where(alive, get(d1, 6), 0.0)
        project(groups, words, unit, x_out, idx_out, u_out, first)
        return 0

    lax.fori_loop(0, (total + 15) >> 4, two_groups, 0)


def first_kernel(
    live, send, local, velocity, properties,
    x_out, idx_out, imp_out, u_out, m_out, meta, share, vel, prop, d0, d1, words,
):
    for c in range(6):
        for h in range(HIGH):
            vel[c * HIGH + h : c * HIGH + h + 1, :] = velocity[c : c + 1, h * LANES : (h + 1) * LANES]
    for c in range(4):
        for h in range(HIGH):
            prop[c * HIGH + h : c * HIGH + h + 1, :] = properties[c : c + 1, h * LANES : (h + 1) * LANES]

    def one_partner(q, base):
        count = live[q * BLK]
        for b in range(1, BLK):
            count = count + live[q * BLK + b]
        meta[q] = base
        rows = pl.ds(pl.multiple_of(base * 8, 8), 64)
        d0[rows, :] = send[q]
        d1[rows, :] = local[q]
        return base + ((count + LANES - 1) >> 7)

    total = lax.fori_loop(0, PEERS, one_partner, jnp.int32(0), unroll=4)
    meta[PEERS] = total
    prepare(True, total, d0, d1, vel, prop, words, x_out, idx_out, imp_out, u_out, m_out)

    def one_share(q, _):
        rows = pl.ds(meta[q], 8)
        share[q, 0] = u_out[rows, :]
        share[q, 1] = m_out[rows, :]
        return 0

    lax.fori_loop(0, PEERS, one_share, 0, unroll=8)


def second_kernel(
    arrived, share_first, vel, prop,
    x_out, idx_out, imp_out, u_out, m_out, meta, share, received, d0, words, used, sem, sems,
):
    piece = PEERS // 4
    pieces = []
    for k in range(4):
        part = pl.ds(k * piece, piece)
        pieces.append(pltpu.make_async_copy(arrived.at[part], received.at[part], sems.at[k]))
        pieces[k].start()
    copy = pltpu.make_async_copy(share_first, share.at[:, 0:2], sem)
    copy.start()

    def count_rows(q, _):
        flags = received[q, pl.ds(4, 8, stride=8), :]
        used[q] = jnp.max(jnp.where(flags >= 0.0, row_iota() + 1, 0))
        return 0

    for k in range(4):
        pieces[k].wait()
        lax.fori_loop(k * piece, (k + 1) * piece, count_rows, 0, unroll=8)

    def one_partner(q, base):
        meta[q] = base
        d0[pl.ds(pl.multiple_of(base * 8, 8), 64), :] = received[q]
        return base + used[q]

    total = lax.fori_loop(0, PEERS, one_partner, jnp.int32(0), unroll=4)
    meta[PEERS] = total
    prepare(False, total, d0, None, vel, prop, words, x_out, idx_out, imp_out, u_out, m_out)

    def one_share(q, _):
        rows = pl.ds(meta[q], 8)
        share[q, 2] = u_out[rows, :]
        share[q, 3] = m_out[rows, :]
        return 0

    lax.fori_loop(0, PEERS, one_share, 0, unroll=8)
    copy.wait()


def merge(side, shift, meta_in, ins, outs):
    terms = 6 if side else 7

    def one_group(g, _):
        for c in range(7):
            outs[0][g + shift, c] = ins[0][g, c] if c < terms else jnp.zeros((8, LANES), F32)
        for k in range(1, 5):
            outs[k][group_rows(g + shift), :] = ins[k][group_rows(g), :]
        return 0

    count = (meta_in[PEERS] + 7) >> 3
    lax.fori_loop(0, count, one_group, 0)
    return shift + count


def apply_kernel(start, *refs):
    if start:
        meta_a, meta_b = refs[:2]
        sides = refs[2:7], refs[7:12]
        received, j_out, new, weight, x, idx, meta, imp, u, w, other, mass = refs[12:]
        shift = merge(0, 0, meta_a, sides[0], (x, idx, imp, u, w))
        groups = merge(1, shift, meta_b, sides[1], (x, idx, imp, u, w))
        meta[COUNT] = groups
        zero = jnp.zeros((8, LANES), F32)
        for k in range(CHUNK):
            rows = group_rows(groups + k)
            for c in range(7):
                x[groups + k, c] = zero
            idx[rows, :] = zero.astype(jnp.int32)
            imp[rows, :] = zero
            u[rows, :] = zero
            w[rows, :] = zero - 1.0
    else:
        meta, x, idx, imp, u, weight, received, j_out, new, other = refs
    step = 2 if start else 1

    def one_partner(p, _):
        if start:
            meta[p] = meta_a[p]
            mass[pl.ds(meta[p], 8), :] = received[p, 3]
        other[pl.ds(meta[p], 8), :] = received[p, step]
        return 0

    def second_partner(p, _):
        if start:
            meta[PEERS + p] = meta_b[p] + shift * 8
            mass[pl.ds(meta[PEERS + p], 8), :] = received[p, 1]
        other[pl.ds(meta[PEERS + p], 8), :] = received[p, 0]
        return 0

    lax.fori_loop(0, PEERS, one_partner, 0, unroll=8)
    lax.fori_loop(0, PEERS, second_partner, 0, unroll=8)
    iota_high = lax.broadcasted_iota(jnp.int32, (HIGH, LANES), 0)
    iota_low = lax.broadcasted_iota(jnp.int32, (LANES, LANES), 0)

    def one_chunk(i, total):
        lefts = []
        rights = []
        for j in range(CHUNK):
            g = i * CHUNK + j
            rows = group_rows(g)
            if start:
                mine = w[rows, :]
                alive = mine > 0.0
                scale = jnp.where(alive, relax / (mine + mass[rows, :]), 0.0)
                weight[rows, :] = scale
            else:
                scale = weight[rows, :]
                alive = scale > 0.0
            before = imp[rows, :]
            fresh = jnp.maximum(before - (u[rows, :] + other[rows, :]) * scale, 0.0)
            fresh = jnp.where(alive, fresh, before)
            applied = fresh - before
            new[rows, :] = fresh
            values = [applied * x[g, c] for c in range(6)]
            tops = [v.astype(BF16).astype(F32) for v in values]
            pieces = tops + [v - t for v, t in zip(values, tops)]
            index = idx[rows, :]
            low = index & (LANES - 1)
            high = index >> 7
            for b in range(8):
                mask = jnp.broadcast_to(high[b : b + 1], (HIGH, LANES)) == iota_high
                lefts.append(
                    jnp.concatenate(
                        [
                            jnp.where(mask, jnp.broadcast_to(v[b : b + 1], (HIGH, LANES)), 0.0).astype(BF16)
                            for v in pieces
                        ],
                        axis=0,
                    )
                )
                hit = jnp.broadcast_to(low[b : b + 1], (LANES, LANES)) == iota_low
                rights.append(jnp.where(hit, 1.0, 0.0).astype(BF16))
        return total + lax.dot_general(
            jnp.concatenate(lefts, axis=1),
            jnp.concatenate(rights, axis=1),
            (((1,), (1,)), ((), ())),
            preferred_element_type=F32,
        )

    chunks = (meta[COUNT] + CHUNK - 1) // CHUNK
    total = lax.fori_loop(0, chunks, one_chunk, jnp.zeros((12 * HIGH, LANES), F32))
    j_out[...] = total[0:96] + total[96:192]


def moved(vel, prop, j0, j1, j3, j2, c):
    rows = slice(c * HIGH, (c + 1) * HIGH)
    k = max(c - 2, 0)
    gain = (j0[rows, :] + j1[rows, :]) + (j2[rows, :] + j3[rows, :])
    return vel[rows, :] + prop[k * HIGH : (k + 1) * HIGH, :] * gain


def gather_kernel(meta, vel, prop, j0, j1, j3, j2, x, idx, vel_out, u_out, share, words):
    rows = [moved(vel, prop, j0, j1, j3, j2, c) for c in range(6)]
    for c in range(6):
        vel_out[c * HIGH : (c + 1) * HIGH, :] = rows[c]
    unit = fixed_words(rows, words)

    def two_groups(pair, _):
        project([pair * 2, pair * 2 + 1], words, unit, x, idx, u_out, True)
        return 0

    lax.fori_loop(0, (meta[COUNT] + 1) >> 1, two_groups, 0)

    def one_share(q, _):
        share[q, 0] = u_out[pl.ds(meta[q], 8), :]
        share[q, 1] = u_out[pl.ds(meta[PEERS + q], 8), :]
        return 0

    lax.fori_loop(0, PEERS, one_share, 0, unroll=8)


def final_kernel(vel, prop, j0, j1, j3, j2, out):
    for c in range(6):
        rows = moved(vel, prop, j0, j1, j3, j2, c)
        for h in range(HIGH):
            out[c : c + 1, h * LANES : (h + 1) * LANES] = rows[h : h + 1]


def unpack_kernel(live, meta, imp, warm, out):
    lanes = lax.broadcasted_iota(jnp.int32, (1, LANES), 1)

    def one_partner(q, _):
        offset = jnp.int32(0)
        for b in range(BLK):
            count = live[q * BLK + b]
            shift = offset & (LANES - 1)
            row = meta[q] + (offset >> 7)
            here = imp[pl.ds(row, 1), :]
            after = imp[pl.ds(row + 1, 1), :]
            both = jnp.where(lanes >= shift, here, after)
            back = pltpu.roll(both, (LANES - shift) & (LANES - 1), 1)
            slot = pl.ds(q * BLK + b, 1)
            out[slot, :] = jnp.where(lanes < count, back, warm[slot, :])
            offset = offset + count
        return 0

    lax.fori_loop(0, PEERS, one_partner, 0, unroll=4)


def shape(*dims, dtype=F32):
    return jax.ShapeDtypeStruct(dims, dtype)


def call(kernel, ins, outs, scratch=(), name=None):
    return pl.pallas_call(
        kernel,
        in_specs=list(ins),
        out_specs=tuple(SMEM if o.dtype == jnp.int32 and len(o.shape) == 1 else VMEM for o in outs),
        out_shape=tuple(outs),
        scratch_shapes=list(scratch),
        compiler_params=pltpu.CompilerParams(vmem_limit_bytes=16 << 20),
        cost_estimate=pl.CostEstimate(
            flops=10_000_000, bytes_accessed=4_000_000, transcendentals=0
        ),
        name=name,
    )


def pack(sent, live, geometry, index, value):
    rows = pl.BlockSpec((PART * BLK, LANES), lambda i: (i, 0))
    return pl.pallas_call(
        functools.partial(pack_kernel, sent),
        grid=(PEERS // PART,),
        in_specs=[SMEM, pl.BlockSpec((9, PART * BLK * LANES), lambda i: (0, i)), rows, rows],
        out_specs=pl.BlockSpec((PART, 64, LANES), lambda i: (i, 0, 0)),
        out_shape=shape(PEERS, 64, LANES),
        scratch_shapes=[pltpu.VMEM((64, LANES), F32), pltpu.VMEM((16, 8, LANES), F32)] * WAYS,
        compiler_params=pltpu.CompilerParams(
            dimension_semantics=("arbitrary",), vmem_limit_bytes=(60 if sent else 16) << 20
        ),
        cost_estimate=pl.CostEstimate(
            flops=10_000_000, bytes_accessed=4_000_000, transcendentals=0
        ),
        name="pack_sent" if sent else "pack_local",
    )(live, geometry, index, value)


def on_device(
    velocity, properties, first_body, second_body, geometry, target_speed, warm_impulse, live_pairs
):
    table = lambda array: array.reshape(ROWS, LANES)
    warm = table(warm_impulse)
    words = pltpu.VMEM((64, LANES), jnp.int32)

    def streams(groups, terms, length):
        stream = shape(length, LANES)
        return [
            shape(groups, terms, 8, LANES), shape(length, LANES, dtype=jnp.int32), stream, stream, stream
        ]

    send = pack(True, live_pairs, geometry, table(second_body), warm)
    local = pack(False, live_pairs, geometry, table(first_body), table(target_speed))
    received = lax.all_to_all(send, "owner", split_axis=0, concat_axis=0, tiled=True)
    *side_a, meta_a, share, vel, prop = call(
        first_kernel,
        [SMEM] + [VMEM] * 4,
        streams(ROWS // 8, 7, STAGE)
        + [
            shape(PEERS + 1, dtype=jnp.int32), shape(PEERS, 2, 8, LANES),
            shape(96, LANES), shape(64, LANES),
        ],
        [pltpu.VMEM((STAGE * 8, LANES), F32)] * 2 + [words],
        name="first",
    )(live_pairs, send, local, velocity, properties)
    *side_b, meta_b, share = call(
        second_kernel,
        [pl.BlockSpec(memory_space=pltpu.HBM)] * 2 + [VMEM] * 2,
        streams(ROWS // 8, 6, STAGE)
        + [shape(PEERS + 1, dtype=jnp.int32), shape(PEERS, 4, 8, LANES)],
        [
            pltpu.VMEM((PEERS, 64, LANES), F32), pltpu.VMEM((STAGE * 8, LANES), F32), words,
            pltpu.SMEM((PEERS,), jnp.int32), pltpu.SemaphoreType.DMA, pltpu.SemaphoreType.DMA((4,)),
        ],
        name="second",
    )(received, share, vel, prop)
    n_sub = lax.axis_size("sub")
    stream = shape(STREAM, LANES)
    scratch = pltpu.VMEM((STREAM, LANES), F32)
    for iteration in range(ITERS):
        told = lax.all_to_all(share, "owner", split_axis=0, concat_axis=0, tiled=True)
        if iteration == 0:
            own, imp, weight, x, idx, meta = call(
                functools.partial(apply_kernel, True),
                [SMEM] * 2 + [VMEM] * 11,
                [shape(96, LANES), stream, stream]
                + streams(GROUPS, 7, STREAM)[:2]
                + [shape(COUNT + 1, dtype=jnp.int32)],
                [scratch] * 5,
                name="apply",
            )(meta_a, meta_b, *side_a, *side_b, told)
        else:
            own, imp = call(
                functools.partial(apply_kernel, False),
                [SMEM] + [VMEM] * 6,
                [shape(96, LANES), stream],
                [scratch],
                name="apply",
            )(meta, x, idx, imp, u, weight, told)
        gains = [own] + [
            lax.ppermute(own, "sub", [(i, i ^ d) for i in range(n_sub)]) for d in (1, 3, 2)
        ]
        if iteration < ITERS - 1:
            vel, u, share = call(
                gather_kernel,
                [SMEM] + [VMEM] * 8,
                [shape(96, LANES), stream, shape(PEERS, 2, 8, LANES)],
                [words],
                name="gather",
            )(meta, vel, prop, *gains, x, idx)
    (impulse,) = call(
        unpack_kernel, [SMEM, SMEM, VMEM, VMEM], [shape(ROWS, LANES)], name="unpack"
    )(live_pairs, meta, imp, warm)
    (out,) = call(final_kernel, [VMEM] * 6, [shape(6, HIGH * LANES)], name="final")(
        vel, prop, *gains
    )
    return (out, impulse.reshape(-1))


def solution(mesh):
    return jax.shard_map(
        on_device,
        mesh=mesh,
        in_specs=(
            P(None, "owner"),
            P(None, "owner"),
            P(("owner", "sub")),
            P(("owner", "sub")),
            P(None, ("owner", "sub")),
            P(("owner", "sub")),
            P(("owner", "sub")),
            P(("owner", "sub")),
        ),
        out_specs=(P(None, "owner"), P(("owner", "sub"))),
        check_vma=False,
    )
```

```python
import functools

import jax
import jax.numpy as jnp
from jax import lax
from jax.experimental import pallas as pl
from jax.experimental.pallas import tpu as pltpu
from jax.sharding import PartitionSpec as P

ITERS = 4
relax = 0.1
F32 = jnp.float32
BF16 = jnp.bfloat16
LANES = 128
BLK = 8
PEERS = 32
HIGH = 16
ROWS = PEERS * BLK
STAGE = ROWS + 2 * BLK
HALF = float(1 << 20)
CHUNK = 5
GROUPS = 2 * ROWS // 8 + CHUNK
STREAM = GROUPS * 8
COUNT = 2 * PEERS
PART = 16
WAYS = 4
VMEM = pl.BlockSpec(memory_space=pltpu.VMEM)
SMEM = pl.BlockSpec(memory_space=pltpu.SMEM)


def lane_iota():
    return lax.broadcasted_iota(jnp.int32, (8, LANES), 1)


def row_iota():
    return lax.broadcasted_iota(jnp.int32, (8, LANES), 0)


def pack_kernel(sent, live, geom, index, value, out, *scratch):
    start = pl.program_id(0) * PART
    lanes = lane_iota()
    subs = row_iota()
    fill = jnp.where((subs == 4) & sent, -1.0, 0.0).astype(F32)
    mixes = (subs >= 3) & (subs < 6) if sent else subs >= 6

    def one_partner(q, mixed, packed):
        rows = pl.ds(pl.multiple_of(q * BLK, BLK), BLK)
        mixed[pl.ds(4 if sent else 7, 8, stride=8), :] = (index[rows, :] & (HIGH * LANES - 1)).astype(F32)
        mixed[pl.ds(5 if sent else 6, 8, stride=8), :] = value[rows, :]
        cols = [pl.ds(pl.multiple_of(q * BLK * LANES + b * LANES, LANES), LANES) for b in range(BLK)]
        if sent:
            for b in range(BLK):
                mixed[pl.ds(8 * b + 3, 1), :] = geom[8:9, cols[b]]
        offset = jnp.int32(0)
        current = jnp.zeros((8, LANES), F32)
        for b in range(BLK):
            shift = offset & (LANES - 1)
            row = offset >> 7
            both = jnp.where(mixes, mixed[8 * b : 8 * b + 8, :], geom[0:8, cols[b]])
            rolled = pltpu.roll(both, shift, 1)
            current = jnp.where(lanes < shift, current, rolled)
            packed[row] = current
            offset = offset + live[(start + q) * BLK + b]
            spill = jnp.broadcast_to((offset >> 7) > row, (8, LANES))
            current = jnp.where(spill, rolled, current)
        packed[offset >> 7] = current
        for r in range(BLK):
            out[q, 8 * r : 8 * r + 8, :] = jnp.where(lanes + r * LANES < offset, packed[r], fill)

    def some_partners(step, _):
        for k in range(WAYS):
            one_partner(step * WAYS + k, *scratch[2 * k : 2 * k + 2])
        return 0

    lax.fori_loop(0, PART // WAYS, some_partners, 0)


def gather_rows(tables, index, count):
    lows = [i & (LANES - 1) for i in index]
    highs = [i >> 7 for i in index]
    found = [[None] * count for _ in index]
    for h in range(HIGH):
        masks = [hi == h for hi in highs]
        for c in range(count):
            ref, start = tables[c]
            line = jnp.broadcast_to(ref[start + h : start + h + 1, :], (8, LANES))
            for k in range(len(index)):
                got = jnp.take_along_axis(line, lows[k], axis=1, mode="promise_in_bounds")
                found[k][c] = got if h == 0 else jnp.where(masks[k], got, found[k][c])
    return found


def group_rows(g):
    return pl.ds(pl.multiple_of(g * 8, 8), 8)


def fixed_words(rows, words):
    most = jnp.abs(rows[0])
    for part in rows[1:]:
        most = jnp.maximum(most, jnp.abs(part))
    most = jnp.max(jnp.max(most, axis=0, keepdims=True), axis=1, keepdims=True)
    most = jnp.maximum(jnp.broadcast_to(most, (HIGH, LANES)), 1e-30)
    scale = (HALF - 2.0) / most
    whole = [(part * scale + (HALF + 0.5)).astype(jnp.int32) for part in rows]
    for k in range(4):
        extra = whole[4 + k // 2]
        extra = extra >> 11 if k % 2 else extra & 2047
        words[k * HIGH : (k + 1) * HIGH, :] = whole[k] | (extra << 21)
    return most[0:8] * (1.0 / (HALF - 2.0))


def project(groups, words, unit, x, idx, u_out, offset):
    rows = [group_rows(g) for g in groups]
    got = gather_rows([(words, HIGH * k) for k in range(4)], [idx[r, :] for r in rows], 4)
    for k, g in enumerate(groups):
        tops = [lax.shift_right_logical(w, 21) for w in got[k]]
        whole = [w & ((1 << 21) - 1) for w in got[k]]
        whole += [tops[0] | (tops[1] << 11), tops[2] | (tops[3] << 11)]
        u = jnp.zeros((8, LANES), F32)
        for c in range(6):
            u = u + x[g, c] * (whole[c] - (1 << 20)).astype(F32)
        u = u * unit
        u_out[rows[k], :] = u - x[g, 6] if offset else u


def prepare(first, total, unit, d0, d1, prop, words, x_out, idx_out, imp_out, u_out, m_out):

    def load(g):
        base = g * 64

        def get(ref, k):
            return ref[pl.ds(base + k, 8, stride=8), :]

        flag = get(d0, 4)
        alive = (flag >= 0.0) & (row_iota() + g * 8 < total)
        source, arms, index = (d1, (3, 4, 5), get(d1, 7)) if first else (d0, (6, 7, 3), flag)
        normal = [get(source, k) for k in (0, 1, 2)]
        arm = [get(source, k) for k in arms]
        cross = [
            arm[1] * normal[2] - arm[2] * normal[1],
            arm[2] * normal[0] - arm[0] * normal[2],
            arm[0] * normal[1] - arm[1] * normal[0],
        ]
        return get, alive, jnp.where(alive, index, 0.0).astype(jnp.int32), normal, cross

    def two_groups(pair, _):
        groups = [pair * 2, pair * 2 + 1]
        indices = [load(g)[2] for g in groups]
        masses = gather_rows([(prop, HIGH * c) for c in range(4)], indices, 4)
        for k, g in enumerate(groups):
            get, alive, index, normal, cross = load(g)
            mass = masses[k][0]
            for c in range(3):
                mass = mass + cross[c] * cross[c] * masses[k][1 + c]
            rows = group_rows(g)
            m_out[rows, :] = jnp.where(alive, mass, -1.0)
            idx_out[rows, :] = index
            imp_out[rows, :] = jnp.where(alive, get(d0, 5), 0.0)
            sign = 1.0 if first else -1.0
            for c, term in enumerate(normal + cross):
                x_out[g, c] = jnp.where(alive, sign * term, 0.0)
            if first:
                x_out[g, 6] = jnp.where(alive, get(d1, 6), 0.0)
        project(groups, words, unit, x_out, idx_out, u_out, first)
        return 0

    lax.fori_loop(0, (total + 15) >> 4, two_groups, 0)


def first_kernel(
    live, send, local, velocity, properties,
    x_out, idx_out, imp_out, u_out, m_out, meta, share, vel, prop, d0, d1, words,
):
    for c in range(6):
        for h in range(HIGH):
            vel[c * HIGH + h : c * HIGH + h + 1, :] = velocity[c : c + 1, h * LANES : (h + 1) * LANES]
    for c in range(4):
        for h in range(HIGH):
            prop[c * HIGH + h : c * HIGH + h + 1, :] = properties[c : c + 1, h * LANES : (h + 1) * LANES]

    def one_partner(q, base):
        count = live[q * BLK]
        for b in range(1, BLK):
            count = count + live[q * BLK + b]
        meta[q] = base
        rows = pl.ds(pl.multiple_of(base * 8, 8), 64)
        d0[rows, :] = send[q]
        d1[rows, :] = local[q]
        return base + ((count + LANES - 1) >> 7)

    total = lax.fori_loop(0, PEERS, one_partner, jnp.int32(0), unroll=4)
    meta[PEERS] = total
    unit = fixed_words([vel[c * HIGH : (c + 1) * HIGH, :] for c in range(6)], words)
    prepare(True, total, unit, d0, d1, prop, words, x_out, idx_out, imp_out, u_out, m_out)

    def one_share(q, _):
        rows = pl.ds(meta[q], 8)
        share[q, 0] = u_out[rows, :]
        share[q, 1] = m_out[rows, :]
        return 0

    lax.fori_loop(0, PEERS, one_share, 0, unroll=8)


def second_kernel(
    arrived, share_first, vel, prop,
    x_out, idx_out, imp_out, u_out, m_out, meta, share, received, d0, words, used, sem, sems,
):
    piece = PEERS // 4
    pieces = []
    for k in range(4):
        part = pl.ds(k * piece, piece)
        pieces.append(pltpu.make_async_copy(arrived.at[part], received.at[part], sems.at[k]))
        pieces[k].start()
    unit = fixed_words([vel[c * HIGH : (c + 1) * HIGH, :] for c in range(6)], words)
    copy = pltpu.make_async_copy(share_first, share.at[:, 0:2], sem)
    copy.start()

    def count_rows(q, _):
        flags = received[q, pl.ds(4, 8, stride=8), :]
        used[q] = jnp.max(jnp.where(flags >= 0.0, row_iota() + 1, 0))
        return 0

    for k in range(4):
        pieces[k].wait()
        lax.fori_loop(k * piece, (k + 1) * piece, count_rows, 0, unroll=8)

    def one_partner(q, base):
        meta[q] = base
        d0[pl.ds(pl.multiple_of(base * 8, 8), 64), :] = received[q]
        return base + used[q]

    total = lax.fori_loop(0, PEERS, one_partner, jnp.int32(0), unroll=4)
    meta[PEERS] = total
    prepare(False, total, unit, d0, None, prop, words, x_out, idx_out, imp_out, u_out, m_out)

    def one_share(q, _):
        rows = pl.ds(meta[q], 8)
        share[q, 2] = u_out[rows, :]
        share[q, 3] = m_out[rows, :]
        return 0

    lax.fori_loop(0, PEERS, one_share, 0, unroll=8)
    copy.wait()


def merge(side, shift, meta_in, ins, outs):
    terms = 6 if side else 7

    def one_group(g, _):
        for c in range(7):
            outs[0][g + shift, c] = ins[0][g, c] if c < terms else jnp.zeros((8, LANES), F32)
        for k in range(1, 5):
            outs[k][group_rows(g + shift), :] = ins[k][group_rows(g), :]
        return 0

    count = (meta_in[PEERS] + 7) >> 3
    lax.fori_loop(0, count, one_group, 0)
    return shift + count


def apply_kernel(start, *refs):
    if start:
        meta_a, meta_b = refs[:2]
        sides = refs[2:7], refs[7:12]
        received, j_out, new, weight, x, idx, meta, imp, u, w, other, mass = refs[12:]
        shift = merge(0, 0, meta_a, sides[0], (x, idx, imp, u, w))
        groups = merge(1, shift, meta_b, sides[1], (x, idx, imp, u, w))
        meta[COUNT] = groups
        zero = jnp.zeros((8, LANES), F32)
        for k in range(CHUNK):
            rows = group_rows(groups + k)
            for c in range(7):
                x[groups + k, c] = zero
            idx[rows, :] = zero.astype(jnp.int32)
            imp[rows, :] = zero
            u[rows, :] = zero
            w[rows, :] = zero - 1.0
    else:
        meta, x, idx, imp, u, weight, received, j_out, new, other = refs
    step = 2 if start else 1

    def one_partner(p, _):
        if start:
            meta[p] = meta_a[p]
            mass[pl.ds(meta[p], 8), :] = received[p, 3]
        other[pl.ds(meta[p], 8), :] = received[p, step]
        return 0

    def second_partner(p, _):
        if start:
            meta[PEERS + p] = meta_b[p] + shift * 8
            mass[pl.ds(meta[PEERS + p], 8), :] = received[p, 1]
        other[pl.ds(meta[PEERS + p], 8), :] = received[p, 0]
        return 0

    lax.fori_loop(0, PEERS, one_partner, 0, unroll=8)
    lax.fori_loop(0, PEERS, second_partner, 0, unroll=8)
    iota_high = lax.broadcasted_iota(jnp.int32, (HIGH, LANES), 0)
    iota_low = lax.broadcasted_iota(jnp.int32, (LANES, LANES), 0)

    def one_chunk(i, total):
        lefts = []
        rights = []
        for j in range(CHUNK):
            g = i * CHUNK + j
            rows = group_rows(g)
            if start:
                mine = w[rows, :]
                alive = mine > 0.0
                scale = jnp.where(alive, relax / (mine + mass[rows, :]), 0.0)
                weight[rows, :] = scale
            else:
                scale = weight[rows, :]
                alive = scale > 0.0
            before = imp[rows, :]
            fresh = jnp.maximum(before - (u[rows, :] + other[rows, :]) * scale, 0.0)
            fresh = jnp.where(alive, fresh, before)
            applied = fresh - before
            new[rows, :] = fresh
            values = [applied * x[g, c] for c in range(6)]
            tops = [v.astype(BF16).astype(F32) for v in values]
            pieces = tops + [v - t for v, t in zip(values, tops)]
            index = idx[rows, :]
            low = index & (LANES - 1)
            high = index >> 7
            for b in range(8):
                mask = jnp.broadcast_to(high[b : b + 1], (HIGH, LANES)) == iota_high
                lefts.append(
                    jnp.concatenate(
                        [
                            jnp.where(mask, jnp.broadcast_to(v[b : b + 1], (HIGH, LANES)), 0.0).astype(BF16)
                            for v in pieces
                        ],
                        axis=0,
                    )
                )
                hit = jnp.broadcast_to(low[b : b + 1], (LANES, LANES)) == iota_low
                rights.append(jnp.where(hit, 1.0, 0.0).astype(BF16))
        return total + lax.dot_general(
            jnp.concatenate(lefts, axis=1),
            jnp.concatenate(rights, axis=1),
            (((1,), (1,)), ((), ())),
            preferred_element_type=F32,
        )

    chunks = (meta[COUNT] + CHUNK - 1) // CHUNK
    total = lax.fori_loop(0, chunks, one_chunk, jnp.zeros((12 * HIGH, LANES), F32))
    j_out[...] = total[0:96] + total[96:192]


def moved(vel, prop, j0, j1, j3, j2, c):
    rows = slice(c * HIGH, (c + 1) * HIGH)
    k = max(c - 2, 0)
    gain = (j0[rows, :] + j1[rows, :]) + (j2[rows, :] + j3[rows, :])
    return vel[rows, :] + prop[k * HIGH : (k + 1) * HIGH, :] * gain


def gather_kernel(meta, vel, prop, j0, j1, j3, j2, x, idx, vel_out, u_out, share, words):
    rows = [moved(vel, prop, j0, j1, j3, j2, c) for c in range(6)]
    for c in range(6):
        vel_out[c * HIGH : (c + 1) * HIGH, :] = rows[c]
    unit = fixed_words(rows, words)

    def two_groups(pair, _):
        project([pair * 2, pair * 2 + 1], words, unit, x, idx, u_out, True)
        return 0

    lax.fori_loop(0, (meta[COUNT] + 1) >> 1, two_groups, 0)

    def one_share(q, _):
        share[q, 0] = u_out[pl.ds(meta[q], 8), :]
        share[q, 1] = u_out[pl.ds(meta[PEERS + q], 8), :]
        return 0

    lax.fori_loop(0, PEERS, one_share, 0, unroll=8)


def final_kernel(vel, prop, j0, j1, j3, j2, out):
    for c in range(6):
        rows = moved(vel, prop, j0, j1, j3, j2, c)
        for h in range(HIGH):
            out[c : c + 1, h * LANES : (h + 1) * LANES] = rows[h : h + 1]


def unpack_kernel(live, meta, imp, warm, out):
    lanes = lax.broadcasted_iota(jnp.int32, (1, LANES), 1)

    def one_partner(q, _):
        offset = jnp.int32(0)
        for b in range(BLK):
            count = live[q * BLK + b]
            shift = offset & (LANES - 1)
            row = meta[q] + (offset >> 7)
            here = imp[pl.ds(row, 1), :]
            after = imp[pl.ds(row + 1, 1), :]
            both = jnp.where(lanes >= shift, here, after)
            back = pltpu.roll(both, (LANES - shift) & (LANES - 1), 1)
            slot = pl.ds(q * BLK + b, 1)
            out[slot, :] = jnp.where(lanes < count, back, warm[slot, :])
            offset = offset + count
        return 0

    lax.fori_loop(0, PEERS, one_partner, 0, unroll=4)


def shape(*dims, dtype=F32):
    return jax.ShapeDtypeStruct(dims, dtype)


def call(kernel, ins, outs, scratch=(), name=None):
    return pl.pallas_call(
        kernel,
        in_specs=list(ins),
        out_specs=tuple(SMEM if o.dtype == jnp.int32 and len(o.shape) == 1 else VMEM for o in outs),
        out_shape=tuple(outs),
        scratch_shapes=list(scratch),
        compiler_params=pltpu.CompilerParams(vmem_limit_bytes=16 << 20),
        cost_estimate=pl.CostEstimate(
            flops=10_000_000, bytes_accessed=4_000_000, transcendentals=0
        ),
        name=name,
    )


def pack(sent, live, geometry, index, value):
    rows = pl.BlockSpec((PART * BLK, LANES), lambda i: (i, 0))
    return pl.pallas_call(
        functools.partial(pack_kernel, sent),
        grid=(PEERS // PART,),
        in_specs=[SMEM, pl.BlockSpec((9, PART * BLK * LANES), lambda i: (0, i)), rows, rows],
        out_specs=pl.BlockSpec((PART, 64, LANES), lambda i: (i, 0, 0)),
        out_shape=shape(PEERS, 64, LANES),
        scratch_shapes=[pltpu.VMEM((64, LANES), F32), pltpu.VMEM((16, 8, LANES), F32)] * WAYS,
        compiler_params=pltpu.CompilerParams(
            dimension_semantics=("arbitrary",), vmem_limit_bytes=(60 if sent else 16) << 20
        ),
        cost_estimate=pl.CostEstimate(
            flops=10_000_000, bytes_accessed=4_000_000, transcendentals=0
        ),
        name="pack_sent" if sent else "pack_local",
    )(live, geometry, index, value)


def on_device(
    velocity, properties, first_body, second_body, geometry, target_speed, warm_impulse, live_pairs
):
    table = lambda array: array.reshape(ROWS, LANES)
    warm = table(warm_impulse)
    words = pltpu.VMEM((64, LANES), jnp.int32)

    def streams(groups, terms, length):
        stream = shape(length, LANES)
        return [
            shape(groups, terms, 8, LANES), shape(length, LANES, dtype=jnp.int32), stream, stream, stream
        ]

    send = pack(True, live_pairs, geometry, table(second_body), warm)
    local = pack(False, live_pairs, geometry, table(first_body), table(target_speed))
    received = lax.all_to_all(send, "owner", split_axis=0, concat_axis=0, tiled=True)
    *side_a, meta_a, share, vel, prop = call(
        first_kernel,
        [SMEM] + [VMEM] * 4,
        streams(ROWS // 8, 7, STAGE)
        + [
            shape(PEERS + 1, dtype=jnp.int32), shape(PEERS, 2, 8, LANES),
            shape(96, LANES), shape(64, LANES),
        ],
        [pltpu.VMEM((STAGE * 8, LANES), F32)] * 2 + [words],
        name="first",
    )(live_pairs, send, local, velocity, properties)
    *side_b, meta_b, share = call(
        second_kernel,
        [pl.BlockSpec(memory_space=pltpu.HBM)] * 2 + [VMEM] * 2,
        streams(ROWS // 8, 6, STAGE)
        + [shape(PEERS + 1, dtype=jnp.int32), shape(PEERS, 4, 8, LANES)],
        [
            pltpu.VMEM((PEERS, 64, LANES), F32), pltpu.VMEM((STAGE * 8, LANES), F32), words,
            pltpu.SMEM((PEERS,), jnp.int32), pltpu.SemaphoreType.DMA, pltpu.SemaphoreType.DMA((4,)),
        ],
        name="second",
    )(received, share, vel, prop)
    n_sub = lax.axis_size("sub")
    stream = shape(STREAM, LANES)
    scratch = pltpu.VMEM((STREAM, LANES), F32)
    for iteration in range(ITERS):
        told = lax.all_to_all(share, "owner", split_axis=0, concat_axis=0, tiled=True)
        if iteration == 0:
            own, imp, weight, x, idx, meta = call(
                functools.partial(apply_kernel, True),
                [SMEM] * 2 + [VMEM] * 11,
                [shape(96, LANES), stream, stream]
                + streams(GROUPS, 7, STREAM)[:2]
                + [shape(COUNT + 1, dtype=jnp.int32)],
                [scratch] * 5,
                name="apply",
            )(meta_a, meta_b, *side_a, *side_b, told)
        else:
            own, imp = call(
                functools.partial(apply_kernel, False),
                [SMEM] + [VMEM] * 6,
                [shape(96, LANES), stream],
                [scratch],
                name="apply",
            )(meta, x, idx, imp, u, weight, told)
        gains = [own] + [
            lax.ppermute(own, "sub", [(i, i ^ d) for i in range(n_sub)]) for d in (1, 3, 2)
        ]
        if iteration < ITERS - 1:
            vel, u, share = call(
                gather_kernel,
                [SMEM] + [VMEM] * 8,
                [shape(96, LANES), stream, shape(PEERS, 2, 8, LANES)],
                [words],
                name="gather",
            )(meta, vel, prop, *gains, x, idx)
    (impulse,) = call(
        unpack_kernel, [SMEM, SMEM, VMEM, VMEM], [shape(ROWS, LANES)], name="unpack"
    )(live_pairs, meta, imp, warm)
    (out,) = call(final_kernel, [VMEM] * 6, [shape(6, HIGH * LANES)], name="final")(
        vel, prop, *gains
    )
    return (out, impulse.reshape(-1))


def solution(mesh):
    return jax.shard_map(
        on_device,
        mesh=mesh,
        in_specs=(
            P(None, "owner"),
            P(None, "owner"),
            P(("owner", "sub")),
            P(("owner", "sub")),
            P(None, ("owner", "sub")),
            P(("owner", "sub")),
            P(("owner", "sub")),
            P(("owner", "sub")),
        ),
        out_specs=(P(None, "owner"), P(("owner", "sub"))),
        check_vma=False,
    )
```
